32 devices in a mesh: wide: 16 (over z, y, x), narrow: 2 (over core).
Axes of the slice: x: 2, y: 2, z: 4, core: 2. Of those that a mesh axis runs over, the one named last changes fastest.
Arguments:
- pressure: float32 [128, 128, 512], P('wide', 'narrow'), may hold values from -6 to 6
Outputs:
- detail_one: float32 [7, 64, 64, 256], P(None, 'wide', 'narrow')
- detail_two: float32 [7, 32, 32, 128], P(None, 'wide', 'narrow')
- detail_three: float32 [7, 16, 16, 64], P(None, 'wide', 'narrow')
- bands_four: float32 [8, 8, 8, 32], P(None, None, 'narrow')
The draws below stay inside these ranges and needn't reach their ends.
All inputs are finite; a program needn't handle non-finite values.
Results may differ from the reference program's by a relative error of at most 0.00016.
Values sent between devices are 32-bit elements; how exact they have to be, the bound alone decides.
No kernel may reach another device: no remote copies, remote signals or barrier semaphores. Data moves between devices by JAX's collectives and lax.ppermute only.
A program may use at most 64 MiB of HBM per device.

```python
import jax
import jax.numpy as jnp
from jax import lax

COLS = 512
LEVELS = 4
NZ = 128
NY = 128


def block_scale(key, extent, pieces, least, largest):
    gain, own = 1.0, jax.random.fold_in(key, 6)
    for axis_at, blocks in pieces:
        heights = jnp.exp(jax.random.uniform(jax.random.fold_in(own, axis_at), (blocks,), jnp.float32, least / len(pieces), largest / len(pieces)))
        gain = gain * jnp.repeat(heights, extent[axis_at] // blocks).reshape([-1 if axis == axis_at else 1 for axis in range(len(extent))])
    return gain


def gaussian(stream_key, dims, spread, bound, split=(), kind=jnp.bfloat16):
    result = jax.random.normal(stream_key, dims, jnp.float32) * spread
    if len(split) > 0:
        result = block_scale(stream_key, dims, split, -0.22, 0.18) * result
    return jnp.clip(result, min=-bound, max=bound).astype(kind)


def setup_inputs(seed: int = 0) -> dict:
    key_list = jax.random.split(jax.random.key(seed), 2)
    pressure = gaussian(key_list[0], (NZ, NY, COLS), 1.0, 6.0, ((0, 16), (1, 2)), jnp.float32)
    return {"pressure": pressure}


LIFT_ALPHA = -1.586134342
LIFT_BETA = -0.05298011854
LIFT_GAMMA = 0.8829110762
LIFT_DELTA = 0.4435068522
LIFT_ZETA = 1.149604398
LIFT_INVERSE = 1.0 / 1.149604398


def lift_line(volume, along):
    length = volume.shape[along]
    half = length // 2
    even_part = lax.slice_in_dim(volume, 0, length, 2, along)
    odd_part = lax.slice_in_dim(volume, 1, length, 2, along)

    def next_even(source):
        return jnp.concatenate([lax.slice_in_dim(source, 1, half, 1, along), lax.slice_in_dim(source, half - 1, half, 1, along)], along)

    def prev_odd(source):
        return jnp.concatenate([lax.slice_in_dim(source, 0, 1, 1, along), lax.slice_in_dim(source, 0, half - 1, 1, along)], along)

    odd_part = odd_part + LIFT_ALPHA * (even_part + next_even(even_part))
    even_part = even_part + LIFT_BETA * (prev_odd(odd_part) + odd_part)
    odd_part = odd_part + LIFT_GAMMA * (even_part + next_even(even_part))
    even_part = even_part + LIFT_DELTA * (prev_odd(odd_part) + odd_part)
    return jnp.stack([even_part * LIFT_ZETA, odd_part * LIFT_INVERSE], 0)


def one_level(volume):
    x_pair = lift_line(volume, 2)
    y_pair = lift_line(x_pair, 2)
    z_pair = lift_line(y_pair, 2)
    return z_pair.reshape((8,) + z_pair.shape[3:])


def reference(pressure):
    volume = pressure
    details = []
    band_set = None
    for _ in range(LEVELS):
        band_set = one_level(volume)
        details.append(band_set[1:])
        volume = band_set[0]
    return details[0], details[1], details[2], band_set
```

```python
import numpy as np

import jax
import jax.numpy as jnp
from jax import lax
from jax.experimental import pallas as pl
from jax.experimental.pallas import tpu as pltpu
from jax.sharding import PartitionSpec as P

ALPHA = -1.586134342
BETA = -0.05298011854
GAMMA = 0.8829110762
DELTA = 0.4435068522
ZETA = 1.149604398

LANES = 128
SUB = 8
HALO = 16
EDGE = 4
BASE = 24
F32 = jnp.float32
VMEM = pl.BlockSpec(memory_space=pltpu.VMEM)


def lift_table(size):
    cells = np.eye(size)
    even, odd = cells[:, 0::2].copy(), cells[:, 1::2].copy()

    def ahead(v):
        return np.concatenate([v[:, 1:], v[:, -1:]], 1)

    def behind(v):
        return np.concatenate([v[:, :1], v[:, :-1]], 1)

    odd += ALPHA * (even + ahead(even))
    even += BETA * (behind(odd) + odd)
    odd += GAMMA * (even + ahead(even))
    even += DELTA * (behind(odd) + odd)
    return np.concatenate([even * ZETA, odd / ZETA], 1)


def lift_taps():
    table = lift_table(32)
    low, high = table[:, 8], table[:, 16 + 8]
    return [float(low[16 + t]) for t in range(5)], [float(high[17 + t]) for t in range(4)]


LOW, HIGH = lift_taps()


def split(table):
    whole = jnp.asarray(table, F32)
    top = whole.astype(jnp.bfloat16)
    return top, (whole - top.astype(F32)).astype(jnp.bfloat16)


def np_split(table):
    import ml_dtypes

    whole = np.asarray(table, np.float32)
    top = whole.astype(ml_dtypes.bfloat16)
    rest = (whole - top.astype(np.float32)).astype(ml_dtypes.bfloat16)
    return jnp.asarray(top), jnp.asarray(rest)


def halves(v):
    top = v.astype(jnp.bfloat16)
    return top, (v - top.astype(F32)).astype(jnp.bfloat16)


def dot3(v, th, tl):
    top, rest = v
    return (
        jnp.dot(top, th, preferred_element_type=F32)
        + jnp.dot(top, tl, preferred_element_type=F32)
        + jnp.dot(rest, th, preferred_element_type=F32)
    )


def taps_low(at):
    return LOW[0] * at(0) + (
        (LOW[1] * (at(-1) + at(1)) + LOW[2] * (at(-2) + at(2)))
        + (LOW[3] * (at(-3) + at(3)) + LOW[4] * (at(-4) + at(4)))
    )


def taps_high(at):
    return (HIGH[0] * at(1) + HIGH[1] * (at(0) + at(2))) + (
        HIGH[2] * (at(-1) + at(3)) + HIGH[3] * (at(-2) + at(4))
    )


def z_right(s, d):
    return d[-1] + ALPHA * s[-1], s[-1] + BETA * (d[-2] + ALPHA * (s[-2] + s[-1]))


def z_left(s, d):
    return s[0], d[0] + ALPHA * (s[0] + s[1])


def z_lift(s, d, left, right, first, last):
    m = len(s)
    s0p = jnp.where(last, s[-1], right[0])
    d1 = [d[i] + ALPHA * (s[i] + (s[i + 1] if i + 1 < m else s0p)) for i in range(m)]
    d1m = jnp.where(first, d1[0], left[0] + ALPHA * s[0])
    s1 = [s[i] + BETA * ((d1[i - 1] if i else d1m) + d1[i]) for i in range(m)]
    s1p = jnp.where(last, s1[-1], s0p + BETA * (d1[-1] + right[1]))
    d2 = [d1[i] + GAMMA * (s1[i] + (s1[i + 1] if i + 1 < m else s1p)) for i in range(m)]
    s1m = left[1] + BETA * d1m
    d2m = jnp.where(first, d2[0], d1m + GAMMA * (s1m + s1[0]))
    s2 = [s1[i] + DELTA * ((d2[i - 1] if i else d2m) + d2[i]) for i in range(m)]
    return [v * ZETA for v in s2], [v * (1.0 / ZETA) for v in d2]


def place(axis):
    me, count = lax.axis_index(axis), lax.axis_size(axis)
    return me, me == 0, me == count - 1


def xy_one(*refs, one_halo):
    n_halo = 1 if one_halo else 2
    x_ref, halo_refs = refs[0], refs[1 : 1 + n_halo]
    th_ref, tl_ref, ll_ref, d_ref, le_ref, lo_ref, de_ref, do_ref, xs = refs[1 + n_halo :]
    nz, ny, nx = x_ref.shape
    cl = nx // LANES // 2
    own = ny // 2
    _, first, last = place("narrow")
    even = lax.rem(lax.axis_index("wide"), 2) == 0

    def spread(value, rows, starts):
        parts = halves(value.reshape(nz * rows, nx))
        step = 2 * LANES
        for n in range(0, nx, step):
            got = dot3(parts, th_ref[:, n : n + step], tl_ref[:, n : n + step])
            got = got.reshape(nz, rows, step)
            for k in range(step // LANES):
                for start in starts:
                    xs[:, n // LANES + k, start : start + rows, :] = got[:, :, k * LANES : (k + 1) * LANES]

    spread(x_ref[...], ny, (BASE,))
    top, bottom = BASE - HALO, BASE + ny
    if one_halo:
        spread(halo_refs[0][...], HALO, (top, bottom))
    else:
        spread(halo_refs[0][...], HALO, (top,))
        spread(halo_refs[1][...], HALO, (bottom,))

    @pl.when(first)
    def _():
        for t in range(1, 13):
            upto = cl if t > EDGE else 2 * cl
            xs[:, :upto, BASE - t : BASE - t + 1, :] = xs[:, :upto, BASE + t : BASE + t + 1, :]

    end = BASE + ny - 1

    @pl.when(last)
    def _():
        for t in range(1, EDGE + 1):
            xs[:, :, end + t : end + t + 1, :] = xs[:, :, end - t : end - t + 1, :]

    upper = lax.broadcasted_iota(jnp.int32, (SUB, LANES), 0) < EDGE

    @pl.loop(0, nz)
    def _(p):
        for c in range(cl):

            def rows(chunk, start, n):
                return lambda t: xs[p, chunk, pl.ds(start + t, n, stride=2), :]

            ll_ref[p, c, :own, :] = taps_low(rows(c, BASE, own))
            below = taps_low(rows(c, BASE + ny, SUB))
            above = taps_low(rows(c, BASE - 2 * SUB, SUB))
            ll_ref[p, c, own : own + SUB, :] = jnp.where(upper, below, above)
            d_ref[0, p, c] = taps_low(rows(cl + c, BASE, own))
            d_ref[1, p, c] = taps_high(rows(c, BASE, own))
            d_ref[2, p, c] = taps_high(rows(cl + c, BASE, own))

    @pl.when(last)
    def _():
        for t in range(1, EDGE + 1):
            at = own - 1
            ll_ref[:, :, at + t : at + t + 1, :] = ll_ref[:, :, at - t : at - t + 1, :]

    def edges(plane):
        s = [plane(0), plane(2), plane(nz - 4), plane(nz - 2)]
        d = [plane(1), None, plane(nz - 3), plane(nz - 1)]
        return z_right(s, d), z_left(s, d)

    for c in range(cl):
        right, left = edges(lambda k: ll_ref[k, c])
        for j in range(2):
            le_ref[j, c] = jnp.where(even, right[j], left[j])
            lo_ref[j, c] = jnp.where(even, left[j], right[j])
        for b in range(3):
            right, left = edges(lambda k: d_ref[b, k, c])
            for j in range(2):
                de_ref[b, j, c] = jnp.where(even, right[j], left[j])
                do_ref[b, j, c] = jnp.where(even, left[j], right[j])


def xy_two(ll_ref, re_ref, ro_ref, de_ref, do_ref, th_ref, tl_ref, g_ref, d2_ref, h_ref, pe_ref, po_ref, lw, ys):
    nz, cl, tall, _ = ll_ref.shape
    own = tall - SUB
    m = nz // 2
    half = own // 2
    me, first, last = place("wide")
    even = lax.rem(me, 2) == 0
    for c in range(cl):
        s = [ll_ref[2 * i, c] for i in range(m)]
        d = [ll_ref[2 * i + 1, c] for i in range(m)]
        left = [jnp.where(even, ro_ref[j, c], re_ref[j, c]) for j in range(2)]
        right = [jnp.where(even, re_ref[j, c], ro_ref[j, c]) for j in range(2)]
        low, high = z_lift(s, d, left, right, first, last)
        for i in range(m):
            lw[i, :, c * LANES : (c + 1) * LANES] = low[i]
            h_ref[i, c] = high[i][:own]
    got = dot3(halves(lw[...].reshape(m * tall, cl * LANES)), th_ref[...], tl_ref[...])
    got = got.reshape(m, tall, 2 * LANES)
    for xb in range(2):
        part = got[:, :, xb * LANES : (xb + 1) * LANES]
        ys[:, xb, SUB : SUB + own, :] = part[:, :own]
        ys[:, xb, :SUB, :] = part[:, own:]
        ys[:, xb, SUB + own : 2 * SUB + own, :] = part[:, own:]
    for i in range(m):

        def rows(xb):
            return lambda t: ys[i, xb, pl.ds(SUB + t, half, stride=2), :]

        g_ref[i] = taps_low(rows(0))
        d2_ref[0, i] = taps_low(rows(1))
        d2_ref[1, i] = taps_high(rows(0))
        d2_ref[2, i] = taps_high(rows(1))
    lead = de_ref.shape[0] * de_ref.shape[1] * de_ref.shape[2] * own
    pe_ref[:lead] = de_ref[...].reshape(lead, LANES)
    po_ref[:lead] = do_ref[...].reshape(lead, LANES)
    for b in range(3):
        s = [d2_ref[b, 2 * i] for i in range(m // 2)]
        d = [d2_ref[b, 2 * i + 1] for i in range(m // 2)]
        right, left = z_right(s, d), z_left(s, d)
        for j in range(2):
            at = lead + (b * 2 + j) * half
            pe_ref[at : at + half] = jnp.where(even, right[j], left[j])
            po_ref[at : at + half] = jnp.where(even, left[j], right[j])


def z_one(d_ref, re_ref, ro_ref, h_ref, out_ref):
    _, nz, cl, own, _ = d_ref.shape
    m = nz // 2
    me, first, last = place("wide")
    even = lax.rem(me, 2) == 0
    for c in range(cl):
        lanes = slice(c * LANES, (c + 1) * LANES)
        for i in range(m):
            out_ref[3, i, :, lanes] = h_ref[i, c]
        for b in range(3):
            s = [d_ref[b, 2 * i, c] for i in range(m)]
            d = [d_ref[b, 2 * i + 1, c] for i in range(m)]
            at = [((b * 2 + j) * cl + c) * own for j in range(2)]
            got_e = [re_ref[k : k + own] for k in at]
            got_o = [ro_ref[k : k + own] for k in at]
            left = [jnp.where(even, got_o[j], got_e[j]) for j in range(2)]
            right = [jnp.where(even, got_e[j], got_o[j]) for j in range(2)]
            low, high = z_lift(s, d, left, right, first, last)
            for i in range(m):
                out_ref[b, i, :, lanes] = low[i]
                out_ref[4 + b, i, :, lanes] = high[i]


def mirrored(j, size):
    if isinstance(j, int):
        return -j if j < 0 else (2 * (size - 1) - j if j >= size else j)
    return jnp.where(j < 0, -j, jnp.where(j >= size, 2 * (size - 1) - j, j))


def z_deep(*refs, slots):
    got_refs = refs[: len(slots)]
    d2_ref, re_ref, ro_ref, out_ref, zz_ref, seq, low2, low3 = refs[len(slots) :]
    m = d2_ref.shape[1]
    half = d2_ref.shape[2]
    me, first, last = place("wide")
    even = lax.rem(me, 2) == 0
    for ref, offsets in zip(got_refs, slots):
        for k, offset in enumerate(offsets):
            chip = lax.bitwise_xor(me, offset)
            piece = ref[k] if len(ref.shape) == 4 else ref[...]
            seq[pl.ds(chip * m, m)] = piece
    size = seq.shape[0]

    def at_of(ref, size, i):
        return lambda t: ref[mirrored(2 * i + t, size)]

    for i in range(size // 2):
        low2[i] = taps_low(at_of(seq, size, i))
    lead = re_ref.shape[0] - 6 * half
    for i in range(m // 2):
        out_ref[3, i] = taps_high(at_of(seq, size, me * (m // 2) + i))
    for b in range(3):
        s = [d2_ref[b, 2 * i] for i in range(m // 2)]
        d = [d2_ref[b, 2 * i + 1] for i in range(m // 2)]
        at = [lead + (b * 2 + j) * half for j in range(2)]
        got_e = [re_ref[k : k + half] for k in at]
        got_o = [ro_ref[k : k + half] for k in at]
        left = [jnp.where(even, got_o[j], got_e[j]) for j in range(2)]
        right = [jnp.where(even, got_e[j], got_o[j]) for j in range(2)]
        low, high = z_lift(s, d, left, right, first, last)
        for i in range(m // 2):
            out_ref[b, i] = low[i]
            out_ref[4 + b, i] = high[i]
    size2 = size // 2
    for i in range(size2 // 2):
        low3[i] = taps_low(at_of(low2, size2, i))
    own3 = m // 4
    size3 = size2 // 2
    for i in range(own3):
        zz_ref[i] = low3[me * own3 + i]
        zz_ref[own3 + i] = taps_high(at_of(low2, size2, me * own3 + i))
    for i in range(size3 // 2):
        zz_ref[2 * own3 + i] = taps_low(at_of(low3, size3, i))
        zz_ref[2 * own3 + size3 // 2 + i] = taps_high(at_of(low3, size3, i))


def pick(me, value, count):
    rows = value.shape[0] // count
    out = value[:rows]
    for k in range(1, count):
        out = jnp.where(me == k, value[k * rows : (k + 1) * rows], out)
    return out


def xy_deep(*refs, pair, own3):
    if pair:
        zz_ref, other_ref = refs[:2]
    else:
        zz_ref = refs[0]
    th3, tl3, th4, tl4, three_ref, four_ref, xs, ys = refs[2 if pair else 1 :]
    me = lax.axis_index("narrow")
    count = lax.axis_size("narrow")
    planes, rows = zz_ref.shape[-3], zz_ref.shape[-2]
    full = rows * count

    def put(value, start):
        a = 2 * own3
        got = dot3(halves(value[:a].reshape(a * rows, LANES)), th3[...], tl3[...])
        xs[:a, pl.ds(start, rows), :] = got.reshape(a, rows, LANES)
        b = planes - a
        got = dot3(halves(value[a:].reshape(b * rows, LANES)), th4[...], tl4[...])
        xs[a:, pl.ds(start, rows), :] = got.reshape(b, rows, LANES)

    if pair:
        put(zz_ref[...], pl.multiple_of(SUB + rows * me, SUB))
        put(other_ref[...], pl.multiple_of(SUB + rows * (1 - me), SUB))
    else:
        for k in range(count):
            put(zz_ref[k], SUB + rows * k)

    def fold(ref, size):
        end = SUB + size - 1
        for t in range(1, EDGE + 1):
            ref[:, SUB - t : SUB - t + 1, :] = ref[:, SUB + t : SUB + t + 1, :]
            ref[:, end + t : end + t + 1, :] = ref[:, end - t : end - t + 1, :]

    fold(xs, full)
    n3 = full // 2
    wide3 = three_ref.shape[-1]
    for k in range(2 * own3):
        bz, i = k // own3, k % own3
        at = lambda t: xs[k, pl.ds(SUB + t, n3, stride=2), :]
        for by, taps in enumerate((taps_low, taps_high)):
            mine = pick(me, taps(at), count)
            for bx in range(2):
                band = 4 * bz + 2 * by + bx
                if band:
                    three_ref[band - 1, i] = mine[:, bx * wide3 : (bx + 1) * wide3]
    for k in range(2 * own3, planes):
        at = lambda t: xs[k, pl.ds(SUB + t, n3, stride=2), :]
        ys[k - 2 * own3, SUB : SUB + n3, :] = taps_low(at)
    fold(ys, n3)
    n4 = n3 // 2
    wide4 = four_ref.shape[-1]
    deep = (planes - 2 * own3) // 2
    for k in range(2 * deep):
        bz, i = k // deep, k % deep
        at = lambda t: ys[k, pl.ds(SUB + t, n4, stride=2), :]
        for by, taps in enumerate((taps_low, taps_high)):
            mine = pick(me, taps(at), count)
            for bx in range(2):
                four_ref[4 * bz + 2 * by + bx, i] = mine[:, bx * wide4 : (bx + 1) * wide4]


def call(kernel, outs, scratch, name, cost=2_000_000):
    return pl.pallas_call(
        kernel,
        out_shape=tuple(jax.ShapeDtypeStruct(shape, F32) for shape in outs),
        out_specs=tuple(VMEM for _ in outs),
        scratch_shapes=[pltpu.VMEM(shape, F32) for shape in scratch],
        cost_estimate=pl.CostEstimate(flops=cost, bytes_accessed=cost, transcendentals=0),
        name=name,
    )


def wide_swap(value, partner):
    count = lax.axis_size("wide")
    return lax.ppermute(value, "wide", [(i, partner(i)) for i in range(count) if 0 <= partner(i) < count])


def even_pair(i):
    return i ^ 1


def odd_pair(i):
    return ((i + 1) ^ 1) - 1


def xor_pair(mask):
    return lambda i: i ^ mask


def gather_stages(count):
    bits = count.bit_length() - 1
    stages = []
    while bits > 0:
        take = 2 if bits >= 2 else 1
        bits -= take
        stages.append([k << bits for k in range(1, 1 << take)])
    return stages


def per_device(pressure):
    nz, ny, nx = pressure.shape
    count_y = lax.axis_size("narrow")
    count_z = lax.axis_size("wide")
    cl = nx // 2 // LANES
    own = ny // 2
    head, tail = pressure[:, :HALO], pressure[:, ny - HALO :]
    if count_y == 2:
        edge = jnp.where(lax.axis_index("narrow") == 0, tail, head)
        halos = (lax.ppermute(edge, "narrow", [(0, 1), (1, 0)]),)
    else:
        halos = (
            lax.ppermute(tail, "narrow", [(i, i + 1) for i in range(count_y - 1)]),
            lax.ppermute(head, "narrow", [(i + 1, i) for i in range(count_y - 1)]),
        )
    table = lift_table(nx)
    ll, d, le, lo, de, do = call(
        lambda *refs: xy_one(*refs, one_halo=count_y == 2),
        [
            (nz, cl, own + SUB, LANES),
            (3, nz, cl, own, LANES),
            (2, cl, own + SUB, LANES),
            (2, cl, own + SUB, LANES),
            (3, 2, cl, own, LANES),
            (3, 2, cl, own, LANES),
        ],
        [(nz, 2 * cl, ny + 2 * BASE, LANES)],
        "xy_one",
    )(pressure, *halos, *np_split(table))
    re, ro = wide_swap(le, even_pair), wide_swap(lo, odd_pair)
    m, half = nz // 2, own // 2
    rows = 6 * cl * own + 6 * half
    g, d2, h, pe, po = call(
        xy_two,
        [
            (m, half, LANES),
            (3, m, half, LANES),
            (m, cl, own, LANES),
            (rows, LANES),
            (rows, LANES),
        ],
        [(m, own + SUB, cl * LANES), (m, 2, own + 2 * SUB, LANES)],
        "xy_two",
    )(ll, re, ro, de, do, *np_split(lift_table(nx // 2)))
    pieces, slots = [g], [[0]]
    stages = gather_stages(count_z)
    for n, masks in enumerate(stages):
        if n:
            whole = jnp.concatenate([p.reshape((-1, m, half, LANES)) for p in pieces], 0)
            flat = [o for part in slots for o in part]
        else:
            whole, flat = g, [0]
        pieces = [whole] + [wide_swap(whole, xor_pair(mask)) for mask in masks]
        slots = [flat] + [[o ^ mask for o in flat] for mask in masks]
    re2, ro2 = wide_swap(pe, even_pair), wide_swap(po, odd_pair)
    (detail_one,) = call(z_one, [(7, m, own, cl * LANES)], [], "z_one")(d, re2, ro2, h)
    size = m * count_z
    own3 = m // 4
    planes = 2 * own3 + size // 4
    detail_two, zz = call(
        lambda *refs: z_deep(*refs, slots=slots),
        [(7, m // 2, half, LANES), (planes, half, LANES)],
        [(size, half, LANES), (size // 2, half, LANES), (size // 4, half, LANES)],
        "z_deep",
    )(*pieces, d2, re2, ro2)
    table3 = lift_table(nx // 4)
    table4 = table3[:, : nx // 8] @ lift_table(nx // 8)
    table4 = np.concatenate([table4, np.zeros((nx // 4, LANES - nx // 8))], 1)
    if count_y == 2:
        rest = (zz, lax.ppermute(zz, "narrow", [(0, 1), (1, 0)]))
    else:
        rest = (lax.all_gather(zz, "narrow"),)
    full = half * count_y
    detail_three, bands_four = call(
        lambda *refs: xy_deep(*refs, pair=count_y == 2, own3=own3),
        [(7, own3, half // 2, nx // 8), (8, size // 8, half // 4, nx // 16)],
        [(planes, full + 2 * SUB, LANES), (planes - 2 * own3, full // 2 + 2 * SUB, LANES)],
        "xy_deep",
    )(*rest, *np_split(table3), *np_split(table4))
    return detail_one, detail_two, detail_three, bands_four


def solution(mesh):
    in_specs = (P("wide", "narrow", None),)
    out_specs = (
        P(None, "wide", "narrow", None),
        P(None, "wide", "narrow", None),
        P(None, "wide", "narrow", None),
        P(None, None, "narrow", None),
    )
    return jax.shard_map(per_device, mesh=mesh, in_specs=in_specs, out_specs=out_specs, check_vma=False)
```

```python
import numpy as np

import jax
import jax.numpy as jnp
from jax import lax
from jax.experimental import pallas as pl
from jax.experimental.pallas import tpu as pltpu
from jax.sharding import PartitionSpec as P


ALPHA = -1.586134342
BETA = -0.05298011854
GAMMA = 0.8829110762
DELTA = 0.4435068522
ZETA = 1.149604398

LANES = 128
SUB = 8
HALO = 16
PARTS = 2
EDGE = 4
BASE = 24
F32 = jnp.float32
VMEM_LIMIT = 16 * 1024 * 1024
VMEM = pl.BlockSpec(memory_space=pltpu.VMEM)


def lift_table(size):
    cells = np.eye(size)
    even, odd = cells[:, 0::2].copy(), cells[:, 1::2].copy()

    def ahead(v):
        return np.concatenate([v[:, 1:], v[:, -1:]], 1)

    def behind(v):
        return np.concatenate([v[:, :1], v[:, :-1]], 1)

    odd += ALPHA * (even + ahead(even))
    even += BETA * (behind(odd) + odd)
    odd += GAMMA * (even + ahead(even))
    even += DELTA * (behind(odd) + odd)
    return np.concatenate([even * ZETA, odd / ZETA], 1)


def lift_taps():
    table = lift_table(32)
    low, high = table[:, 8], table[:, 16 + 8]
    return [float(low[16 + t]) for t in range(5)], [float(high[17 + t]) for t in range(4)]


LOW, HIGH = lift_taps()


def np_split(table):
    import ml_dtypes

    whole = np.asarray(table, np.float32)
    top = whole.astype(ml_dtypes.bfloat16)
    rest = (whole - top.astype(np.float32)).astype(ml_dtypes.bfloat16)
    return jnp.asarray(top), jnp.asarray(rest)


def halves(v):
    top = v.astype(jnp.bfloat16)
    return top, (v - top.astype(F32)).astype(jnp.bfloat16)


def dot3(v, th, tl):
    top, rest = v
    return (
        jnp.dot(top, th, preferred_element_type=F32)
        + jnp.dot(top, tl, preferred_element_type=F32)
        + jnp.dot(rest, th, preferred_element_type=F32)
    )


def taps_low(at):
    return LOW[0] * at(0) + (
        (LOW[1] * (at(-1) + at(1)) + LOW[2] * (at(-2) + at(2)))
        + (LOW[3] * (at(-3) + at(3)) + LOW[4] * (at(-4) + at(4)))
    )


def taps_high(at):
    return (HIGH[0] * at(1) + HIGH[1] * (at(0) + at(2))) + (
        HIGH[2] * (at(-1) + at(3)) + HIGH[3] * (at(-2) + at(4))
    )


def z_right(s, d):
    return d[-1] + ALPHA * s[-1], s[-1] + BETA * (d[-2] + ALPHA * (s[-2] + s[-1]))


def z_left(s, d):
    return s[0], d[0] + ALPHA * (s[0] + s[1])


def z_lift(s, d, left, right, first, last):
    m = len(s)
    s0p = jnp.where(last, s[-1], right[0])
    d1 = [d[i] + ALPHA * (s[i] + (s[i + 1] if i + 1 < m else s0p)) for i in range(m)]
    d1m = jnp.where(first, d1[0], left[0] + ALPHA * s[0])
    s1 = [s[i] + BETA * ((d1[i - 1] if i else d1m) + d1[i]) for i in range(m)]
    s1p = jnp.where(last, s1[-1], s0p + BETA * (d1[-1] + right[1]))
    d2 = [d1[i] + GAMMA * (s1[i] + (s1[i + 1] if i + 1 < m else s1p)) for i in range(m)]
    s1m = left[1] + BETA * d1m
    d2m = jnp.where(first, d2[0], d1m + GAMMA * (s1m + s1[0]))
    s2 = [s1[i] + DELTA * ((d2[i - 1] if i else d2m) + d2[i]) for i in range(m)]
    return [v * ZETA for v in s2], [v * (1.0 / ZETA) for v in d2]


def place(axis):
    me, count = lax.axis_index(axis), lax.axis_size(axis)
    return me, me == 0, me == count - 1


def spread(value, th_ref, tl_ref, store):
    nz, rows, nx = value.shape
    parts = halves(value.reshape(nz * rows, nx))
    step = 2 * LANES
    for n in range(0, nx, step):
        got = dot3(parts, th_ref[:, n : n + step], tl_ref[:, n : n + step]).reshape(nz, rows, step)
        for k in range(step // LANES):
            store(n // LANES + k, got[:, :, k * LANES : (k + 1) * LANES])


def x_one(x_hbm, th_hbm, tl_hbm, xs, th_ref, tl_ref, xv, sems):
    nz, ny, _ = xv.shape
    part = nz // PARTS
    tables = [
        pltpu.make_async_copy(th_hbm, th_ref, sems.at[PARTS]),
        pltpu.make_async_copy(tl_hbm, tl_ref, sems.at[PARTS + 1]),
    ]
    pieces = [
        pltpu.make_async_copy(x_hbm.at[pl.ds(k * part, part)], xv.at[pl.ds(k * part, part)], sems.at[k])
        for k in range(PARTS)
    ]
    for copy in [pieces[0]] + tables + pieces[1:]:
        copy.start()
    for copy in tables:
        copy.wait()
    for k in range(PARTS):
        pieces[k].wait()
        planes = slice(k * part, (k + 1) * part)

        def store(chunk, block):
            xs[planes, chunk, BASE : BASE + ny, :] = block

        spread(xv[planes], th_ref, tl_ref, store)


def xy_one(*refs, one_halo):
    n_halo = 1 if one_halo else 2
    x_ref, halo_refs = refs[0], refs[1 : 1 + n_halo]
    th_ref, tl_ref, xs, ll_ref, d_ref, le_ref, lo_ref, de_ref, do_ref = refs[1 + n_halo :]
    nz, chunks, tall, _ = x_ref.shape
    ny = tall - 2 * BASE
    cl = chunks // 2
    own = ny // 2
    _, first, last = place("narrow")
    even = lax.rem(lax.axis_index("wide"), 2) == 0

    top, bottom = BASE - HALO, BASE + ny

    def store_at(starts):
        def store(chunk, block):
            for start in starts:
                xs[:, chunk, start : start + HALO, :] = block

        return store

    if one_halo:
        begin = pl.multiple_of(jnp.where(first, 0, ny - HALO), HALO)
        spread(halo_refs[0][:, pl.ds(begin, HALO), :], th_ref, tl_ref, store_at((top, bottom)))
    else:
        spread(halo_refs[0][...], th_ref, tl_ref, store_at((top,)))
        spread(halo_refs[1][...], th_ref, tl_ref, store_at((bottom,)))

    @pl.when(first)
    def _():
        for t in range(1, 13):
            upto = cl if t > EDGE else 2 * cl
            xs[:, :upto, BASE - t : BASE - t + 1, :] = xs[:, :upto, BASE + t : BASE + t + 1, :]

    end = BASE + ny - 1

    @pl.when(last)
    def _():
        for t in range(1, EDGE + 1):
            xs[:, :, end + t : end + t + 1, :] = xs[:, :, end - t : end - t + 1, :]

    upper = lax.broadcasted_iota(jnp.int32, (SUB, LANES), 0) < EDGE

    @pl.loop(0, nz)
    def _(p):
        for c in range(cl):

            def rows(chunk, start, n):
                return lambda t: xs[p, chunk, pl.ds(start + t, n, stride=2), :]

            ll_ref[p, c, :own, :] = taps_low(rows(c, BASE, own))
            below = taps_low(rows(c, BASE + ny, SUB))
            above = taps_low(rows(c, BASE - 2 * SUB, SUB))
            ll_ref[p, c, own : own + SUB, :] = jnp.where(upper, below, above)
            d_ref[0, p, c] = taps_low(rows(cl + c, BASE, own))
            d_ref[1, p, c] = taps_high(rows(c, BASE, own))
            d_ref[2, p, c] = taps_high(rows(cl + c, BASE, own))

    @pl.when(last)
    def _():
        for t in range(1, EDGE + 1):
            at = own - 1
            ll_ref[:, :, at + t : at + t + 1, :] = ll_ref[:, :, at - t : at - t + 1, :]

    def edges(plane):
        s = [plane(0), plane(2), plane(nz - 4), plane(nz - 2)]
        d = [plane(1), None, plane(nz - 3), plane(nz - 1)]
        return z_right(s, d), z_left(s, d)

    for c in range(cl):
        right, left = edges(lambda k: ll_ref[k, c])
        for j in range(2):
            le_ref[j, c] = jnp.where(even, right[j], left[j])
            lo_ref[j, c] = jnp.where(even, left[j], right[j])
        for b in range(3):
            right, left = edges(lambda k: d_ref[b, k, c])
            for j in range(2):
                de_ref[b, j, c] = jnp.where(even, right[j], left[j])
                do_ref[b, j, c] = jnp.where(even, left[j], right[j])


def xy_two(ll_ref, re_ref, ro_ref, th_ref, tl_ref, g_ref, d2_ref, h_ref, pe_ref, po_ref, lw, ys):
    nz, cl, tall, _ = ll_ref.shape
    own = tall - SUB
    m = nz // 2
    half = own // 2
    me, first, last = place("wide")
    even = lax.rem(me, 2) == 0
    for c in range(cl):
        s = [ll_ref[2 * i, c] for i in range(m)]
        d = [ll_ref[2 * i + 1, c] for i in range(m)]
        left = [jnp.where(even, ro_ref[j, c], re_ref[j, c]) for j in range(2)]
        right = [jnp.where(even, re_ref[j, c], ro_ref[j, c]) for j in range(2)]
        low, high = z_lift(s, d, left, right, first, last)
        for i in range(m):
            lw[i, :, c * LANES : (c + 1) * LANES] = low[i]
            h_ref[i, c] = high[i][:own]
    got = dot3(halves(lw[...].reshape(m * tall, cl * LANES)), th_ref[...], tl_ref[...])
    got = got.reshape(m, tall, 2 * LANES)
    for xb in range(2):
        part = got[:, :, xb * LANES : (xb + 1) * LANES]
        ys[:, xb, SUB : SUB + own, :] = part[:, :own]
        ys[:, xb, :SUB, :] = part[:, own:]
        ys[:, xb, SUB + own : 2 * SUB + own, :] = part[:, own:]
    for i in range(m):

        def rows(xb):
            return lambda t: ys[i, xb, pl.ds(SUB + t, half, stride=2), :]

        g_ref[i] = taps_low(rows(0))
        d2_ref[0, i] = taps_low(rows(1))
        d2_ref[1, i] = taps_high(rows(0))
        d2_ref[2, i] = taps_high(rows(1))
    for b in range(3):
        s = [d2_ref[b, 2 * i] for i in range(m // 2)]
        d = [d2_ref[b, 2 * i + 1] for i in range(m // 2)]
        right, left = z_right(s, d), z_left(s, d)
        for j in range(2):
            pe_ref[b, j] = jnp.where(even, right[j], left[j])
            po_ref[b, j] = jnp.where(even, left[j], right[j])


def halo_lift(plane, count, got_e, got_o):
    me, first, last = place("wide")
    even = lax.rem(me, 2) == 0
    s = [plane(2 * i) for i in range(count)]
    d = [plane(2 * i + 1) for i in range(count)]
    left = [jnp.where(even, got_o(j), got_e(j)) for j in range(2)]
    right = [jnp.where(even, got_e(j), got_o(j)) for j in range(2)]
    return z_lift(s, d, left, right, first, last)


def z_one(d_ref, re_ref, ro_ref, h_ref, one_ref):
    _, nz, cl, _, _ = d_ref.shape
    m = nz // 2
    for c in range(cl):
        lanes = slice(c * LANES, (c + 1) * LANES)
        for i in range(m):
            one_ref[3, i, :, lanes] = h_ref[i, c]
        for b in range(3):
            low, high = halo_lift(
                lambda k: d_ref[b, k, c], m, lambda j: re_ref[b, j, c], lambda j: ro_ref[b, j, c]
            )
            for i in range(m):
                one_ref[b, i, :, lanes] = low[i]
                one_ref[4 + b, i, :, lanes] = high[i]


def z_two(d_ref, re_ref, ro_ref, h_ref, two_ref):
    m = d_ref.shape[1] // 2
    for i in range(m):
        two_ref[3, i] = h_ref[i]
    for b in range(3):
        low, high = halo_lift(lambda k: d_ref[b, k], m, lambda j: re_ref[b, j], lambda j: ro_ref[b, j])
        for i in range(m):
            two_ref[b, i] = low[i]
            two_ref[4 + b, i] = high[i]


def mirrored(j, size):
    if isinstance(j, int):
        return -j if j < 0 else (2 * (size - 1) - j if j >= size else j)
    return jnp.where(j < 0, -j, jnp.where(j >= size, 2 * (size - 1) - j, j))


def z_deep(*refs, slots):
    got_refs = refs[: len(slots)]
    h2_ref, zz_ref, seq, low2, low3 = refs[len(slots) :]
    m = got_refs[0].shape[-3]
    me = lax.axis_index("wide")
    for ref, offsets in zip(got_refs, slots):
        for k, offset in enumerate(offsets):
            chip = lax.bitwise_xor(me, offset)
            piece = ref[k] if len(ref.shape) == 4 else ref[...]
            seq[pl.ds(chip * m, m)] = piece
    size = seq.shape[0]

    def at_of(ref, size, i):
        return lambda t: ref[mirrored(2 * i + t, size)]

    for i in range(size // 2):
        low2[i] = taps_low(at_of(seq, size, i))
    for i in range(m // 2):
        h2_ref[i] = taps_high(at_of(seq, size, me * (m // 2) + i))
    size2 = size // 2
    for i in range(size2 // 2):
        low3[i] = taps_low(at_of(low2, size2, i))
    own3 = m // 4
    size3 = size2 // 2
    for i in range(own3):
        zz_ref[i] = low3[me * own3 + i]
        zz_ref[own3 + i] = taps_high(at_of(low2, size2, me * own3 + i))
    for i in range(size3 // 2):
        zz_ref[2 * own3 + i] = taps_low(at_of(low3, size3, i))
        zz_ref[2 * own3 + size3 // 2 + i] = taps_high(at_of(low3, size3, i))


def pick(me, value, count):
    rows = value.shape[0] // count
    out = value[:rows]
    for k in range(1, count):
        out = jnp.where(me == k, value[k * rows : (k + 1) * rows], out)
    return out


def xy_deep(*refs, pair, own3):
    if pair:
        zz_ref, other_ref = refs[:2]
    else:
        zz_ref = refs[0]
    th3, tl3, th4, tl4, three_ref, four_ref, xs, ys = refs[2 if pair else 1 :]
    me = lax.axis_index("narrow")
    count = lax.axis_size("narrow")
    planes, rows = zz_ref.shape[-3], zz_ref.shape[-2]
    full = rows * count

    def put(value, start):
        a = 2 * own3
        got = dot3(halves(value[:a].reshape(a * rows, LANES)), th3[...], tl3[...])
        xs[:a, pl.ds(start, rows), :] = got.reshape(a, rows, LANES)
        b = planes - a
        got = dot3(halves(value[a:].reshape(b * rows, LANES)), th4[...], tl4[...])
        xs[a:, pl.ds(start, rows), :] = got.reshape(b, rows, LANES)

    if pair:
        put(zz_ref[...], pl.multiple_of(SUB + rows * me, SUB))
        put(other_ref[...], pl.multiple_of(SUB + rows * (1 - me), SUB))
    else:
        for k in range(count):
            put(zz_ref[k], SUB + rows * k)

    def fold(ref, size):
        end = SUB + size - 1
        for t in range(1, EDGE + 1):
            ref[:, SUB - t : SUB - t + 1, :] = ref[:, SUB + t : SUB + t + 1, :]
            ref[:, end + t : end + t + 1, :] = ref[:, end - t : end - t + 1, :]

    fold(xs, full)
    n3 = full // 2
    wide3 = three_ref.shape[-1]
    for k in range(2 * own3):
        bz, i = k // own3, k % own3
        at = lambda t: xs[k, pl.ds(SUB + t, n3, stride=2), :]
        for by, taps in enumerate((taps_low, taps_high)):
            mine = pick(me, taps(at), count)
            for bx in range(2):
                band = 4 * bz + 2 * by + bx
                if band:
                    three_ref[band - 1, i] = mine[:, bx * wide3 : (bx + 1) * wide3]
    for k in range(2 * own3, planes):
        at = lambda t: xs[k, pl.ds(SUB + t, n3, stride=2), :]
        ys[k - 2 * own3, SUB : SUB + n3, :] = taps_low(at)
    fold(ys, n3)
    n4 = n3 // 2
    wide4 = four_ref.shape[-1]
    deep = (planes - 2 * own3) // 2
    for k in range(2 * deep):
        bz, i = k // deep, k % deep
        at = lambda t: ys[k, pl.ds(SUB + t, n4, stride=2), :]
        for by, taps in enumerate((taps_low, taps_high)):
            mine = pick(me, taps(at), count)
            for bx in range(2):
                four_ref[4 * bz + 2 * by + bx, i] = mine[:, bx * wide4 : (bx + 1) * wide4]


def call(kernel, outs, scratch, cost=2_000_000, aliases=None):
    return pl.pallas_call(
        kernel,
        out_shape=tuple(jax.ShapeDtypeStruct(shape, F32) for shape in outs),
        out_specs=tuple(VMEM for _ in outs),
        scratch_shapes=[pltpu.VMEM(shape, F32) for shape in scratch],
        cost_estimate=pl.CostEstimate(flops=cost, bytes_accessed=cost, transcendentals=0),
        compiler_params=pltpu.CompilerParams(vmem_limit_bytes=VMEM_LIMIT),
        input_output_aliases=aliases or {},
    )


def wide_swap(value, partner):
    count = lax.axis_size("wide")
    return lax.ppermute(value, "wide", [(i, partner(i)) for i in range(count) if 0 <= partner(i) < count])


def even_pair(i):
    return i ^ 1


def odd_pair(i):
    return ((i + 1) ^ 1) - 1


def xor_pair(mask):
    return lambda i: i ^ mask


def gather_stages(count):
    bits = count.bit_length() - 1
    stages = []
    while bits > 0:
        take = 2 if bits >= 2 else 1
        bits -= take
        stages.append([k << bits for k in range(1, 1 << take)])
    return stages


def per_device(pressure):
    nz, ny, nx = pressure.shape
    count_y = lax.axis_size("narrow")
    count_z = lax.axis_size("wide")
    cl = nx // 2 // LANES
    own = ny // 2
    if count_y == 2:
        halos = (lax.ppermute(pressure, "narrow", [(0, 1), (1, 0)]),)
    else:
        head, tail = pressure[:, :HALO], pressure[:, ny - HALO :]
        halos = (
            lax.ppermute(tail, "narrow", [(i, i + 1) for i in range(count_y - 1)]),
            lax.ppermute(head, "narrow", [(i + 1, i) for i in range(count_y - 1)]),
        )
    table = np_split(lift_table(nx))
    padded = (nz, 2 * cl, ny + 2 * BASE, LANES)
    hbm = pl.BlockSpec(memory_space=pltpu.HBM)
    x_own, *table = pl.pallas_call(
        x_one,
        out_shape=(jax.ShapeDtypeStruct(padded, F32),)
        + tuple(jax.ShapeDtypeStruct(part.shape, part.dtype) for part in table),
        in_specs=(hbm, hbm, hbm),
        out_specs=(VMEM, VMEM, VMEM),
        scratch_shapes=[pltpu.VMEM((nz, ny, nx), F32), pltpu.SemaphoreType.DMA((PARTS + 2,))],
        cost_estimate=pl.CostEstimate(flops=2_000_000, bytes_accessed=2_000_000, transcendentals=0),
        compiler_params=pltpu.CompilerParams(vmem_limit_bytes=VMEM_LIMIT),
        name="x_one",
    )(*[pltpu.with_memory_space_constraint(v, pltpu.HBM) for v in (pressure, *table)])
    _, ll, d, le, lo, de, do = call(
        lambda *refs: xy_one(*refs, one_halo=count_y == 2),
        [
            padded,
            (nz, cl, own + SUB, LANES),
            (3, nz, cl, own, LANES),
            (2, cl, own + SUB, LANES),
            (2, cl, own + SUB, LANES),
            (3, 2, cl, own, LANES),
            (3, 2, cl, own, LANES),
        ],
        [],
        aliases={0: 0},
    )(x_own, *halos, *table)
    re = wide_swap(le, even_pair)
    ro = wide_swap(lo, odd_pair)
    rde = wide_swap(de, even_pair)
    rdo = wide_swap(do, odd_pair)
    m, half = nz // 2, own // 2
    g, d2, h, pe, po = call(
        xy_two,
        [
            (m, half, LANES),
            (3, m, half, LANES),
            (m, cl, own, LANES),
            (3, 2, half, LANES),
            (3, 2, half, LANES),
        ],
        [(m, own + SUB, cl * LANES), (m, 2, own + 2 * SUB, LANES)],
    )(ll, re, ro, *np_split(lift_table(nx // 2)))
    pieces, slots = [g], [[0]]
    stages = gather_stages(count_z)
    for n, masks in enumerate(stages):
        if n:
            whole = jnp.concatenate([p.reshape((-1, m, half, LANES)) for p in pieces], 0)
            flat = [o for part in slots for o in part]
        else:
            whole, flat = g, [0]
        pieces = [whole]
        for mask in masks:
            pieces.append(wide_swap(whole, xor_pair(mask)))
        slots = [flat] + [[o ^ mask for o in flat] for mask in masks]
    re2 = wide_swap(pe, even_pair)
    ro2 = wide_swap(po, odd_pair)
    size = m * count_z
    own3 = m // 4
    planes = 2 * own3 + size // 4
    h2, zz = call(
        lambda *refs: z_deep(*refs, slots=slots),
        [(m // 2, half, LANES), (planes, half, LANES)],
        [(size, half, LANES), (size // 2, half, LANES), (size // 4, half, LANES)],
    )(*pieces)
    (detail_one,) = call(z_one, [(7, m, own, cl * LANES)], [])(d, rde, rdo, h)
    (detail_two,) = call(z_two, [(7, m // 2, half, LANES)], [])(d2, re2, ro2, h2)
    table3 = lift_table(nx // 4)
    table4 = table3[:, : nx // 8] @ lift_table(nx // 8)
    table4 = np.concatenate([table4, np.zeros((nx // 4, LANES - nx // 8))], 1)
    if count_y == 2:
        rest = (zz, lax.ppermute(zz, "narrow", [(0, 1), (1, 0)]))
    else:
        rest = (lax.all_gather(zz, "narrow"),)
    full = half * count_y
    detail_three, bands_four = call(
        lambda *refs: xy_deep(*refs, pair=count_y == 2, own3=own3),
        [(7, own3, half // 2, nx // 8), (8, size // 8, half // 4, nx // 16)],
        [(planes, full + 2 * SUB, LANES), (planes - 2 * own3, full // 2 + 2 * SUB, LANES)],
    )(*rest, *np_split(table3), *np_split(table4))
    return detail_one, detail_two, detail_three, bands_four


def solution(mesh):
    in_specs = (P("wide", "narrow", None),)
    out_specs = (
        P(None, "wide", "narrow", None),
        P(None, "wide", "narrow", None),
        P(None, "wide", "narrow", None),
        P(None, None, "narrow", None),
    )

    return jax.shard_map(per_device, mesh=mesh, in_specs=in_specs, out_specs=out_specs, check_vma=False)
```

```python
import numpy as np

import jax
import jax.numpy as jnp
from jax import lax
from jax.experimental import pallas as pl
from jax.experimental.pallas import tpu as pltpu
from jax.sharding import PartitionSpec as P


ALPHA = -1.586134342
BETA = -0.05298011854
GAMMA = 0.8829110762
DELTA = 0.4435068522
ZETA = 1.149604398

LANES = 128
SUB = 8
HALO = 16
PARTS = 2
EDGE = 4
BASE = 24
F32 = jnp.float32
VMEM_LIMIT = 16 * 1024 * 1024
VMEM = pl.BlockSpec(memory_space=pltpu.VMEM)


def lift_table(size):
    cells = np.eye(size)
    even, odd = cells[:, 0::2].copy(), cells[:, 1::2].copy()

    def ahead(v):
        return np.concatenate([v[:, 1:], v[:, -1:]], 1)

    def behind(v):
        return np.concatenate([v[:, :1], v[:, :-1]], 1)

    odd += ALPHA * (even + ahead(even))
    even += BETA * (behind(odd) + odd)
    odd += GAMMA * (even + ahead(even))
    even += DELTA * (behind(odd) + odd)
    return np.concatenate([even * ZETA, odd / ZETA], 1)


def lift_taps():
    table = lift_table(32)
    low, high = table[:, 8], table[:, 16 + 8]
    return [float(low[16 + t]) for t in range(5)], [float(high[17 + t]) for t in range(4)]


LOW, HIGH = lift_taps()


def np_split(table):
    import ml_dtypes

    whole = np.asarray(table, np.float32)
    top = whole.astype(ml_dtypes.bfloat16)
    rest = (whole - top.astype(np.float32)).astype(ml_dtypes.bfloat16)
    return jnp.asarray(top), jnp.asarray(rest)


def halves(v):
    top = v.astype(jnp.bfloat16)
    return top, (v - top.astype(F32)).astype(jnp.bfloat16)


def dot3(v, th, tl):
    top, rest = v
    return (
        jnp.dot(top, th, preferred_element_type=F32)
        + jnp.dot(top, tl, preferred_element_type=F32)
        + jnp.dot(rest, th, preferred_element_type=F32)
    )


def taps_low(at):
    return LOW[0] * at(0) + (
        (LOW[1] * (at(-1) + at(1)) + LOW[2] * (at(-2) + at(2)))
        + (LOW[3] * (at(-3) + at(3)) + LOW[4] * (at(-4) + at(4)))
    )


def taps_high(at):
    return (HIGH[0] * at(1) + HIGH[1] * (at(0) + at(2))) + (
        HIGH[2] * (at(-1) + at(3)) + HIGH[3] * (at(-2) + at(4))
    )


def z_right(s, d):
    return d[-1] + ALPHA * s[-1], s[-1] + BETA * (d[-2] + ALPHA * (s[-2] + s[-1]))


def z_left(s, d):
    return s[0], d[0] + ALPHA * (s[0] + s[1])


def z_lift(s, d, left, right, first, last):
    m = len(s)
    s0p = jnp.where(last, s[-1], right[0])
    d1 = [d[i] + ALPHA * (s[i] + (s[i + 1] if i + 1 < m else s0p)) for i in range(m)]
    d1m = jnp.where(first, d1[0], left[0] + ALPHA * s[0])
    s1 = [s[i] + BETA * ((d1[i - 1] if i else d1m) + d1[i]) for i in range(m)]
    s1p = jnp.where(last, s1[-1], s0p + BETA * (d1[-1] + right[1]))
    d2 = [d1[i] + GAMMA * (s1[i] + (s1[i + 1] if i + 1 < m else s1p)) for i in range(m)]
    s1m = left[1] + BETA * d1m
    d2m = jnp.where(first, d2[0], d1m + GAMMA * (s1m + s1[0]))
    s2 = [s1[i] + DELTA * ((d2[i - 1] if i else d2m) + d2[i]) for i in range(m)]
    return [v * ZETA for v in s2], [v * (1.0 / ZETA) for v in d2]


def place(axis):
    me, count = lax.axis_index(axis), lax.axis_size(axis)
    return me, me == 0, me == count - 1


def spread(value, th_ref, tl_ref, store):
    nz, rows, nx = value.shape
    parts = halves(value.reshape(nz * rows, nx))
    step = 2 * LANES
    for n in range(0, nx, step):
        got = dot3(parts, th_ref[:, n : n + step], tl_ref[:, n : n + step]).reshape(nz, rows, step)
        for k in range(step // LANES):
            store(n // LANES + k, got[:, :, k * LANES : (k + 1) * LANES])


def x_one(x_hbm, th_hbm, tl_hbm, xs, th_ref, tl_ref, xv, sems):
    nz, ny, _ = xv.shape
    part = nz // PARTS
    tables = [
        pltpu.make_async_copy(th_hbm, th_ref, sems.at[PARTS]),
        pltpu.make_async_copy(tl_hbm, tl_ref, sems.at[PARTS + 1]),
    ]
    pieces = [
        pltpu.make_async_copy(x_hbm.at[pl.ds(k * part, part)], xv.at[pl.ds(k * part, part)], sems.at[k])
        for k in range(PARTS)
    ]
    for copy in [pieces[0]] + tables + pieces[1:]:
        copy.start()
    for copy in tables:
        copy.wait()
    for k in range(PARTS):
        pieces[k].wait()
        planes = slice(k * part, (k + 1) * part)

        def store(chunk, block):
            xs[planes, chunk, BASE : BASE + ny, :] = block

        spread(xv[planes], th_ref, tl_ref, store)


def xy_one(*refs, one_halo):
    n_halo = 1 if one_halo else 2
    x_ref, halo_refs = refs[0], refs[1 : 1 + n_halo]
    th_ref, tl_ref, xs, ll_ref, d_ref, le_ref, lo_ref, de_ref, do_ref = refs[1 + n_halo :]
    nz, chunks, tall, _ = x_ref.shape
    ny = tall - 2 * BASE
    cl = chunks // 2
    own = ny // 2
    _, first, last = place("narrow")
    even = lax.rem(lax.axis_index("wide"), 2) == 0

    top, bottom = BASE - HALO, BASE + ny

    def store_at(starts):
        def store(chunk, block):
            for start in starts:
                xs[:, chunk, start : start + HALO, :] = block

        return store

    if one_halo:
        begin = pl.multiple_of(jnp.where(first, 0, ny - HALO), HALO)
        spread(halo_refs[0][:, pl.ds(begin, HALO), :], th_ref, tl_ref, store_at((top, bottom)))
    else:
        spread(halo_refs[0][...], th_ref, tl_ref, store_at((top,)))
        spread(halo_refs[1][...], th_ref, tl_ref, store_at((bottom,)))

    @pl.when(first)
    def _():
        for t in range(1, 13):
            upto = cl if t > EDGE else 2 * cl
            xs[:, :upto, BASE - t : BASE - t + 1, :] = xs[:, :upto, BASE + t : BASE + t + 1, :]

    end = BASE + ny - 1

    @pl.when(last)
    def _():
        for t in range(1, EDGE + 1):
            xs[:, :, end + t : end + t + 1, :] = xs[:, :, end - t : end - t + 1, :]

    upper = lax.broadcasted_iota(jnp.int32, (SUB, LANES), 0) < EDGE

    @pl.loop(0, nz)
    def _(p):
        for c in range(cl):

            def rows(chunk, start, n):
                return lambda t: xs[p, chunk, pl.ds(start + t, n, stride=2), :]

            ll_ref[p, c, :own, :] = taps_low(rows(c, BASE, own))
            below = taps_low(rows(c, BASE + ny, SUB))
            above = taps_low(rows(c, BASE - 2 * SUB, SUB))
            ll_ref[p, c, own : own + SUB, :] = jnp.where(upper, below, above)
            d_ref[0, p, c] = taps_low(rows(cl + c, BASE, own))
            d_ref[1, p, c] = taps_high(rows(c, BASE, own))
            d_ref[2, p, c] = taps_high(rows(cl + c, BASE, own))

    @pl.when(last)
    def _():
        for t in range(1, EDGE + 1):
            at = own - 1
            ll_ref[:, :, at + t : at + t + 1, :] = ll_ref[:, :, at - t : at - t + 1, :]

    def edges(plane):
        s = [plane(0), plane(2), plane(nz - 4), plane(nz - 2)]
        d = [plane(1), None, plane(nz - 3), plane(nz - 1)]
        return z_right(s, d), z_left(s, d)

    for c in range(cl):
        right, left = edges(lambda k: ll_ref[k, c])
        for j in range(2):
            le_ref[j, c] = jnp.where(even, right[j], left[j])
            lo_ref[j, c] = jnp.where(even, left[j], right[j])
        for b in range(3):
            right, left = edges(lambda k: d_ref[b, k, c])
            for j in range(2):
                de_ref[b, j, c] = jnp.where(even, right[j], left[j])
                do_ref[b, j, c] = jnp.where(even, left[j], right[j])


def xy_two(ll_ref, re_ref, ro_ref, th_ref, tl_ref, t3h_ref, t3l_ref, g_ref, d2_ref, h_ref, pe_ref, po_ref, lw, ys):
    nz, cl, tall, _ = ll_ref.shape
    own = tall - SUB
    m = nz // 2
    half = own // 2
    me, first, last = place("wide")
    even = lax.rem(me, 2) == 0
    for c in range(cl):
        s = [ll_ref[2 * i, c] for i in range(m)]
        d = [ll_ref[2 * i + 1, c] for i in range(m)]
        left = [jnp.where(even, ro_ref[j, c], re_ref[j, c]) for j in range(2)]
        right = [jnp.where(even, re_ref[j, c], ro_ref[j, c]) for j in range(2)]
        low, high = z_lift(s, d, left, right, first, last)
        for i in range(m):
            lw[i, :, c * LANES : (c + 1) * LANES] = low[i]
            h_ref[i, c] = high[i][:own]
    got = dot3(halves(lw[...].reshape(m * tall, cl * LANES)), th_ref[...], tl_ref[...])
    got = got.reshape(m, tall, 2 * LANES)
    for xb in range(2):
        part = got[:, :, xb * LANES : (xb + 1) * LANES]
        ys[:, xb, SUB : SUB + own, :] = part[:, :own]
        ys[:, xb, :SUB, :] = part[:, own:]
        ys[:, xb, SUB + own : 2 * SUB + own, :] = part[:, own:]
    for i in range(m):

        def rows(xb):
            return lambda t: ys[i, xb, pl.ds(SUB + t, half, stride=2), :]

        d2_ref[0, i] = taps_low(rows(0))
        d2_ref[1, i] = taps_low(rows(1))
        d2_ref[2, i] = taps_high(rows(0))
        d2_ref[3, i] = taps_high(rows(1))
    deeper = dot3(halves(d2_ref[0].reshape(m * half, LANES)), t3h_ref[...], t3l_ref[...])
    g_ref[...] = deeper.reshape(m, half, LANES)
    for b in range(4):
        s = [d2_ref[b, 2 * i] for i in range(m // 2)]
        d = [d2_ref[b, 2 * i + 1] for i in range(m // 2)]
        right, left = z_right(s, d), z_left(s, d)
        for j in range(2):
            pe_ref[b, j] = jnp.where(even, right[j], left[j])
            po_ref[b, j] = jnp.where(even, left[j], right[j])


def halo_lift(plane, count, got_e, got_o):
    me, first, last = place("wide")
    even = lax.rem(me, 2) == 0
    s = [plane(2 * i) for i in range(count)]
    d = [plane(2 * i + 1) for i in range(count)]
    left = [jnp.where(even, got_o(j), got_e(j)) for j in range(2)]
    right = [jnp.where(even, got_e(j), got_o(j)) for j in range(2)]
    return z_lift(s, d, left, right, first, last)


def z_one(d_ref, re_ref, ro_ref, h_ref, one_ref):
    _, nz, cl, _, _ = d_ref.shape
    m = nz // 2
    for c in range(cl):
        lanes = slice(c * LANES, (c + 1) * LANES)
        for i in range(m):
            one_ref[3, i, :, lanes] = h_ref[i, c]
        for b in range(3):
            low, high = halo_lift(
                lambda k: d_ref[b, k, c], m, lambda j: re_ref[b, j, c], lambda j: ro_ref[b, j, c]
            )
            for i in range(m):
                one_ref[b, i, :, lanes] = low[i]
                one_ref[4 + b, i, :, lanes] = high[i]


def z_two(d_ref, re_ref, ro_ref, two_ref):
    m = d_ref.shape[1] // 2
    for b in range(4):
        low, high = halo_lift(lambda k: d_ref[b, k], m, lambda j: re_ref[b, j], lambda j: ro_ref[b, j])
        for i in range(m):
            if b:
                two_ref[b - 1, i] = low[i]
            two_ref[3 + b, i] = high[i]


def near_slot(z, above):
    return jnp.where((lax.rem(z, 2) == 0) == above, 4, 12)


def pack_last(own_ref, four_ref, eight_ref, twelve_ref, px_ref, py_ref):
    me = lax.axis_index("wide")
    z = me // 4
    lanes = lax.broadcasted_iota(jnp.int32, own_ref.shape, 2)
    half = LANES // 2
    for out_ref, bit in ((px_ref, 1), (py_ref, 2)):
        above = lax.rem(me // bit, 2) == 0
        close = near_slot(z, above) == 4
        out_ref[0] = own_ref[...]
        out_ref[1] = jnp.where(close, four_ref[...], twelve_ref[...])
        rest = jnp.where(close, twelve_ref[...], four_ref[...])
        for i in range(own_ref.shape[0]):
            out_ref[2, i] = jnp.where(lanes[i] < half, rest[i], pltpu.roll(eight_ref[i], half, 1))


def mirrored(j, size):
    if isinstance(j, int):
        return -j if j < 0 else (2 * (size - 1) - j if j >= size else j)
    return jnp.where(j < 0, -j, jnp.where(j >= size, 2 * (size - 1) - j, j))


def z_deep(*refs, slots):
    got_refs = refs[: len(slots)]
    t4h_ref, t4l_ref, zz_ref, seq, low2, low3 = refs[len(slots) :]
    m, half = got_refs[0].shape[-3], zz_ref.shape[1]
    me = lax.axis_index("wide")

    def put(offset, piece):
        seq[pl.ds(lax.bitwise_xor(me, offset) * m, m)] = piece

    for ref, offsets in zip(got_refs, slots):
        if isinstance(offsets, int):
            partner = lax.bitwise_xor(me, offsets)
            above = lax.rem(partner // (1 if offsets == 1 else 2), 2) == 0
            slot = near_slot(me // 4, above)
            keep = lax.broadcasted_iota(jnp.int32, (half, LANES), 1) < LANES // 2
            put(offsets, ref[0])
            put(lax.bitwise_xor(slot, offsets), ref[1])
            for k, offset in ((0, lax.bitwise_xor(16 - slot, offsets)), (1, offsets ^ 8)):
                chip = lax.bitwise_xor(me, offset)
                for i in range(m):
                    value = pltpu.roll(ref[2, i], LANES // 2, 1) if k else ref[2, i]
                    seq[chip * m + i] = jnp.where(keep, value, 0.0)
            continue
        for k, offset in enumerate(offsets):
            put(offset, ref[k] if len(ref.shape) == 4 else ref[...])
    size = seq.shape[0]

    def at_of(ref, size, i):
        return lambda t: ref[mirrored(2 * i + t, size)]

    for i in range(size // 2):
        low2[i] = taps_low(at_of(seq, size, i))
    size2 = size // 2
    for i in range(size2 // 2):
        low3[i] = taps_low(at_of(low2, size2, i))
    own3 = m // 4
    size3 = size2 // 2
    for i in range(own3):
        zz_ref[i] = low3[me * own3 + i]
        zz_ref[own3 + i] = taps_high(at_of(low2, size2, me * own3 + i))
    for i in range(size3 // 2):
        seq[i] = taps_low(at_of(low3, size3, i))
        seq[size3 // 2 + i] = taps_high(at_of(low3, size3, i))
    rows = size3 * half
    got = dot3(halves(seq[:size3].reshape(rows, LANES)), t4h_ref[...], t4l_ref[...])
    zz_ref[2 * own3 :] = got.reshape(size3, half, LANES)


def pick(me, value, count):
    rows = value.shape[0] // count
    out = value[:rows]
    for k in range(1, count):
        out = jnp.where(me == k, value[k * rows : (k + 1) * rows], out)
    return out


def xy_deep(*refs, pair, own3):
    if pair:
        zz_ref, other_ref = refs[:2]
    else:
        zz_ref = refs[0]
    three_ref, four_ref, xs, ys = refs[2 if pair else 1 :]
    me = lax.axis_index("narrow")
    count = lax.axis_size("narrow")
    planes, rows = zz_ref.shape[-3], zz_ref.shape[-2]
    full = rows * count

    def put(value, start):
        xs[:, pl.ds(start, rows), :] = value

    if pair:
        put(zz_ref[...], pl.multiple_of(SUB + rows * me, SUB))
        put(other_ref[...], pl.multiple_of(SUB + rows * (1 - me), SUB))
    else:
        for k in range(count):
            put(zz_ref[k], SUB + rows * k)

    def fold(ref, size):
        end = SUB + size - 1
        for t in range(1, EDGE + 1):
            ref[:, SUB - t : SUB - t + 1, :] = ref[:, SUB + t : SUB + t + 1, :]
            ref[:, end + t : end + t + 1, :] = ref[:, end - t : end - t + 1, :]

    fold(xs, full)
    n3 = full // 2
    wide3 = three_ref.shape[-1]
    for k in range(2 * own3):
        bz, i = k // own3, k % own3
        at = lambda t: xs[k, pl.ds(SUB + t, n3, stride=2), :]
        for by, taps in enumerate((taps_low, taps_high)):
            mine = pick(me, taps(at), count)
            for bx in range(2):
                band = 4 * bz + 2 * by + bx
                if band:
                    three_ref[band - 1, i] = mine[:, bx * wide3 : (bx + 1) * wide3]
    for k in range(2 * own3, planes):
        at = lambda t: xs[k, pl.ds(SUB + t, n3, stride=2), :]
        ys[k - 2 * own3, SUB : SUB + n3, :] = taps_low(at)
    fold(ys, n3)
    n4 = n3 // 2
    wide4 = four_ref.shape[-1]
    deep = (planes - 2 * own3) // 2
    for k in range(2 * deep):
        bz, i = k // deep, k % deep
        at = lambda t: ys[k, pl.ds(SUB + t, n4, stride=2), :]
        for by, taps in enumerate((taps_low, taps_high)):
            mine = pick(me, taps(at), count)
            for bx in range(2):
                four_ref[4 * bz + 2 * by + bx, i] = mine[:, bx * wide4 : (bx + 1) * wide4]


def call(kernel, outs, scratch, cost=2_000_000, aliases=None):
    return pl.pallas_call(
        kernel,
        out_shape=tuple(jax.ShapeDtypeStruct(shape, F32) for shape in outs),
        out_specs=tuple(VMEM for _ in outs),
        scratch_shapes=[pltpu.VMEM(shape, F32) for shape in scratch],
        cost_estimate=pl.CostEstimate(flops=cost, bytes_accessed=cost, transcendentals=0),
        compiler_params=pltpu.CompilerParams(vmem_limit_bytes=VMEM_LIMIT),
        input_output_aliases=aliases or {},
    )


def wide_swap(value, partner):
    count = lax.axis_size("wide")
    return lax.ppermute(value, "wide", [(i, partner(i)) for i in range(count) if 0 <= partner(i) < count])


def even_pair(i):
    return i ^ 1


def odd_pair(i):
    return ((i + 1) ^ 1) - 1


def xor_pair(mask):
    return lambda i: i ^ mask


def gather_stages(count):
    bits = count.bit_length() - 1
    stages = []
    while bits > 0:
        take = 2 if bits >= 2 else 1
        bits -= take
        stages.append([k << bits for k in range(1, 1 << take)])
    return stages


def per_device(pressure):
    nz, ny, nx = pressure.shape
    count_y = lax.axis_size("narrow")
    count_z = lax.axis_size("wide")
    cl = nx // 2 // LANES
    own = ny // 2
    if count_y == 2:
        halos = (lax.ppermute(pressure, "narrow", [(0, 1), (1, 0)]),)
    else:
        head, tail = pressure[:, :HALO], pressure[:, ny - HALO :]
        halos = (
            lax.ppermute(tail, "narrow", [(i, i + 1) for i in range(count_y - 1)]),
            lax.ppermute(head, "narrow", [(i + 1, i) for i in range(count_y - 1)]),
        )
    table = np_split(lift_table(nx))
    padded = (nz, 2 * cl, ny + 2 * BASE, LANES)
    hbm = pl.BlockSpec(memory_space=pltpu.HBM)
    x_own, *table = pl.pallas_call(
        x_one,
        out_shape=(jax.ShapeDtypeStruct(padded, F32),)
        + tuple(jax.ShapeDtypeStruct(part.shape, part.dtype) for part in table),
        in_specs=(hbm, hbm, hbm),
        out_specs=(VMEM, VMEM, VMEM),
        scratch_shapes=[pltpu.VMEM((nz, ny, nx), F32), pltpu.SemaphoreType.DMA((PARTS + 2,))],
        cost_estimate=pl.CostEstimate(flops=2_000_000, bytes_accessed=2_000_000, transcendentals=0),
        compiler_params=pltpu.CompilerParams(vmem_limit_bytes=VMEM_LIMIT),
        name="x_one",
    )(*[pltpu.with_memory_space_constraint(v, pltpu.HBM) for v in (pressure, *table)])
    _, ll, d, le, lo, de, do = call(
        lambda *refs: xy_one(*refs, one_halo=count_y == 2),
        [
            padded,
            (nz, cl, own + SUB, LANES),
            (3, nz, cl, own, LANES),
            (2, cl, own + SUB, LANES),
            (2, cl, own + SUB, LANES),
            (3, 2, cl, own, LANES),
            (3, 2, cl, own, LANES),
        ],
        [],
        aliases={0: 0},
    )(x_own, *halos, *table)
    re = wide_swap(le, even_pair)
    ro = wide_swap(lo, odd_pair)
    rde = wide_swap(de, even_pair)
    rdo = wide_swap(do, odd_pair)
    m, half = nz // 2, own // 2
    g, d2, h, pe, po = call(
        xy_two,
        [
            (m, half, LANES),
            (4, m, half, LANES),
            (m, cl, own, LANES),
            (4, 2, half, LANES),
            (4, 2, half, LANES),
        ],
        [(m, own + SUB, cl * LANES), (m, 2, own + 2 * SUB, LANES)],
    )(ll, re, ro, *np_split(lift_table(nx // 2)), *np_split(lift_table(nx // 4)))
    pieces, slots = [g], [[0]]
    stages = gather_stages(count_z)
    for n, masks in enumerate(stages):
        final = n == len(stages) - 1
        if final and count_z == 16:
            block = (3, m, half, LANES)
            px, py = call(pack_last, [block, block], [])(*pieces)
            for mask in masks:
                pieces.append(wide_swap(px if mask == 1 else py, xor_pair(mask)))
                slots.append(mask)
            break
        whole, flat = g, [0]
        if n:
            whole = jnp.concatenate([p.reshape((-1, m, half, LANES)) for p in pieces], 0)
            flat = [o for part in slots for o in part]
        pieces = [whole]
        for mask in masks:
            pieces.append(wide_swap(whole, xor_pair(mask)))
        slots = [flat] + [[o ^ mask for o in flat] for mask in masks]
    re2 = wide_swap(pe, even_pair)
    ro2 = wide_swap(po, odd_pair)
    size = m * count_z
    own3 = m // 4
    planes = 2 * own3 + size // 4
    table4 = np.zeros((LANES, LANES))
    table4[: nx // 8, : nx // 8] = lift_table(nx // 8)
    (zz,) = call(
        lambda *refs: z_deep(*refs, slots=slots),
        [(planes, half, LANES)],
        [(size, half, LANES), (size // 2, half, LANES), (size // 4, half, LANES)],
    )(*pieces, *np_split(table4))
    (detail_one,) = call(z_one, [(7, m, own, cl * LANES)], [])(d, rde, rdo, h)
    (detail_two,) = call(z_two, [(7, m // 2, half, LANES)], [])(d2, re2, ro2)
    if count_y == 2:
        rest = (zz, lax.ppermute(zz, "narrow", [(0, 1), (1, 0)]))
    else:
        rest = (lax.all_gather(zz, "narrow"),)
    full = half * count_y
    detail_three, bands_four = call(
        lambda *refs: xy_deep(*refs, pair=count_y == 2, own3=own3),
        [(7, own3, half // 2, nx // 8), (8, size // 8, half // 4, nx // 16)],
        [(planes, full + 2 * SUB, LANES), (planes - 2 * own3, full // 2 + 2 * SUB, LANES)],
    )(*rest)
    return detail_one, detail_two, detail_three, bands_four


def solution(mesh):
    in_specs = (P("wide", "narrow", None),)
    out_specs = (
        P(None, "wide", "narrow", None),
        P(None, "wide", "narrow", None),
        P(None, "wide", "narrow", None),
        P(None, None, "narrow", None),
    )

    return jax.shard_map(per_device, mesh=mesh, in_specs=in_specs, out_specs=out_specs, check_vma=False)
```

```python
import numpy as np

import jax
import jax.numpy as jnp
from jax import lax
from jax.experimental import pallas as pl
from jax.experimental.pallas import tpu as pltpu
from jax.sharding import PartitionSpec as P


ALPHA = -1.586134342
BETA = -0.05298011854
GAMMA = 0.8829110762
DELTA = 0.4435068522
ZETA = 1.149604398

LANES = 128
SUB = 8
HALO = 16
PARTS = 2
EDGE = 4
BASE = 24
F32 = jnp.float32
VMEM_LIMIT = 16 * 1024 * 1024
VMEM = pl.BlockSpec(memory_space=pltpu.VMEM)


def lift_table(size):
    cells = np.eye(size)
    even, odd = cells[:, 0::2].copy(), cells[:, 1::2].copy()

    def ahead(v):
        return np.concatenate([v[:, 1:], v[:, -1:]], 1)

    def behind(v):
        return np.concatenate([v[:, :1], v[:, :-1]], 1)

    odd += ALPHA * (even + ahead(even))
    even += BETA * (behind(odd) + odd)
    odd += GAMMA * (even + ahead(even))
    even += DELTA * (behind(odd) + odd)
    return np.concatenate([even * ZETA, odd / ZETA], 1)


def lift_taps():
    table = lift_table(32)
    low, high = table[:, 8], table[:, 16 + 8]
    return [float(low[16 + t]) for t in range(5)], [float(high[17 + t]) for t in range(4)]


LOW, HIGH = lift_taps()


def np_split(table):
    import ml_dtypes

    whole = np.asarray(table, np.float32)
    top = whole.astype(ml_dtypes.bfloat16)
    rest = (whole - top.astype(np.float32)).astype(ml_dtypes.bfloat16)
    return jnp.asarray(top), jnp.asarray(rest)


def halves(v):
    top = v.astype(jnp.bfloat16)
    return top, (v - top.astype(F32)).astype(jnp.bfloat16)


def dot3(v, th, tl):
    top, rest = v
    return (
        jnp.dot(top, th, preferred_element_type=F32)
        + jnp.dot(top, tl, preferred_element_type=F32)
        + jnp.dot(rest, th, preferred_element_type=F32)
    )


def taps_low(at):
    return LOW[0] * at(0) + (
        (LOW[1] * (at(-1) + at(1)) + LOW[2] * (at(-2) + at(2)))
        + (LOW[3] * (at(-3) + at(3)) + LOW[4] * (at(-4) + at(4)))
    )


def taps_high(at):
    return (HIGH[0] * at(1) + HIGH[1] * (at(0) + at(2))) + (
        HIGH[2] * (at(-1) + at(3)) + HIGH[3] * (at(-2) + at(4))
    )


def z_right(s, d):
    return d[-1] + ALPHA * s[-1], s[-1] + BETA * (d[-2] + ALPHA * (s[-2] + s[-1]))


def z_left(s, d):
    return s[0], d[0] + ALPHA * (s[0] + s[1])


def z_lift(s, d, left, right, first, last):
    m = len(s)
    s0p = jnp.where(last, s[-1], right[0])
    d1 = [d[i] + ALPHA * (s[i] + (s[i + 1] if i + 1 < m else s0p)) for i in range(m)]
    d1m = jnp.where(first, d1[0], left[0] + ALPHA * s[0])
    s1 = [s[i] + BETA * ((d1[i - 1] if i else d1m) + d1[i]) for i in range(m)]
    s1p = jnp.where(last, s1[-1], s0p + BETA * (d1[-1] + right[1]))
    d2 = [d1[i] + GAMMA * (s1[i] + (s1[i + 1] if i + 1 < m else s1p)) for i in range(m)]
    s1m = left[1] + BETA * d1m
    d2m = jnp.where(first, d2[0], d1m + GAMMA * (s1m + s1[0]))
    s2 = [s1[i] + DELTA * ((d2[i - 1] if i else d2m) + d2[i]) for i in range(m)]
    return [v * ZETA for v in s2], [v * (1.0 / ZETA) for v in d2]


def place(axis):
    me, count = lax.axis_index(axis), lax.axis_size(axis)
    return me, me == 0, me == count - 1


def spread(value, th_ref, tl_ref, store):
    nz, rows, nx = value.shape
    parts = halves(value.reshape(nz * rows, nx))
    step = 2 * LANES
    for n in range(0, nx, step):
        got = dot3(parts, th_ref[:, n : n + step], tl_ref[:, n : n + step]).reshape(nz, rows, step)
        for k in range(step // LANES):
            store(n // LANES + k, got[:, :, k * LANES : (k + 1) * LANES])


def x_one(x_hbm, th_hbm, tl_hbm, xs, th_ref, tl_ref, xv, sems):
    nz, ny, _ = xv.shape
    part = nz // PARTS
    tables = [
        pltpu.make_async_copy(th_hbm, th_ref, sems.at[PARTS]),
        pltpu.make_async_copy(tl_hbm, tl_ref, sems.at[PARTS + 1]),
    ]
    pieces = [
        pltpu.make_async_copy(x_hbm.at[pl.ds(k * part, part)], xv.at[pl.ds(k * part, part)], sems.at[k])
        for k in range(PARTS)
    ]
    for copy in [pieces[0]] + tables + pieces[1:]:
        copy.start()
    for copy in tables:
        copy.wait()
    for k in range(PARTS):
        pieces[k].wait()
        planes = slice(k * part, (k + 1) * part)

        def store(chunk, block):
            xs[planes, chunk, BASE : BASE + ny, :] = block

        spread(xv[planes], th_ref, tl_ref, store)


def xy_one(*refs, one_halo):
    n_halo = 1 if one_halo else 2
    x_ref, halo_refs = refs[0], refs[1 : 1 + n_halo]
    th_ref, tl_ref, xs, ll_ref, d_ref, le_ref, lo_ref, de_ref, do_ref = refs[1 + n_halo :]
    nz, chunks, tall, _ = x_ref.shape
    ny = tall - 2 * BASE
    cl = chunks // 2
    own = ny // 2
    _, first, last = place("narrow")
    even = lax.rem(lax.axis_index("wide"), 2) == 0

    top, bottom = BASE - HALO, BASE + ny

    def store_at(starts):
        def store(chunk, block):
            for start in starts:
                xs[:, chunk, start : start + HALO, :] = block

        return store

    if one_halo:
        begin = pl.multiple_of(jnp.where(first, 0, ny - HALO), HALO)
        spread(halo_refs[0][:, pl.ds(begin, HALO), :], th_ref, tl_ref, store_at((top, bottom)))
    else:
        spread(halo_refs[0][...], th_ref, tl_ref, store_at((top,)))
        spread(halo_refs[1][...], th_ref, tl_ref, store_at((bottom,)))

    @pl.when(first)
    def _():
        for t in range(1, 13):
            upto = cl if t > EDGE else 2 * cl
            xs[:, :upto, BASE - t : BASE - t + 1, :] = xs[:, :upto, BASE + t : BASE + t + 1, :]

    end = BASE + ny - 1

    @pl.when(last)
    def _():
        for t in range(1, EDGE + 1):
            xs[:, :, end + t : end + t + 1, :] = xs[:, :, end - t : end - t + 1, :]

    upper = lax.broadcasted_iota(jnp.int32, (SUB, LANES), 0) < EDGE

    @pl.loop(0, nz)
    def _(p):
        for c in range(cl):

            def rows(chunk, start, n):
                return lambda t: xs[p, chunk, pl.ds(start + t, n, stride=2), :]

            ll_ref[p, c, :own, :] = taps_low(rows(c, BASE, own))
            below = taps_low(rows(c, BASE + ny, SUB))
            above = taps_low(rows(c, BASE - 2 * SUB, SUB))
            ll_ref[p, c, own : own + SUB, :] = jnp.where(upper, below, above)
            d_ref[0, p, c] = taps_low(rows(cl + c, BASE, own))
            d_ref[1, p, c] = taps_high(rows(c, BASE, own))
            d_ref[2, p, c] = taps_high(rows(cl + c, BASE, own))

    @pl.when(last)
    def _():
        for t in range(1, EDGE + 1):
            at = own - 1
            ll_ref[:, :, at + t : at + t + 1, :] = ll_ref[:, :, at - t : at - t + 1, :]

    def edges(plane):
        s = [plane(0), plane(2), plane(nz - 4), plane(nz - 2)]
        d = [plane(1), None, plane(nz - 3), plane(nz - 1)]
        return z_right(s, d), z_left(s, d)

    for c in range(cl):
        right, left = edges(lambda k: ll_ref[k, c])
        for j in range(2):
            le_ref[j, c] = jnp.where(even, right[j], left[j])
            lo_ref[j, c] = jnp.where(even, left[j], right[j])
        for b in range(3):
            right, left = edges(lambda k: d_ref[b, k, c])
            for j in range(2):
                de_ref[b, j, c] = jnp.where(even, right[j], left[j])
                do_ref[b, j, c] = jnp.where(even, left[j], right[j])


def xy_two(ll_ref, re_ref, ro_ref, th_ref, tl_ref, t3h_ref, t3l_ref, g_ref, d2_ref, h_ref, pe_ref, po_ref, lw, ys):
    nz, cl, tall, _ = ll_ref.shape
    own = tall - SUB
    m = nz // 2
    half = own // 2
    me, first, last = place("wide")
    even = lax.rem(me, 2) == 0
    for c in range(cl):
        s = [ll_ref[2 * i, c] for i in range(m)]
        d = [ll_ref[2 * i + 1, c] for i in range(m)]
        left = [jnp.where(even, ro_ref[j, c], re_ref[j, c]) for j in range(2)]
        right = [jnp.where(even, re_ref[j, c], ro_ref[j, c]) for j in range(2)]
        low, high = z_lift(s, d, left, right, first, last)
        for i in range(m):
            lw[i, :, c * LANES : (c + 1) * LANES] = low[i]
            h_ref[i, c] = high[i][:own]
    got = dot3(halves(lw[...].reshape(m * tall, cl * LANES)), th_ref[...], tl_ref[...])
    got = got.reshape(m, tall, 2 * LANES)
    for xb in range(2):
        part = got[:, :, xb * LANES : (xb + 1) * LANES]
        ys[:, xb, SUB : SUB + own, :] = part[:, :own]
        ys[:, xb, :SUB, :] = part[:, own:]
        ys[:, xb, SUB + own : 2 * SUB + own, :] = part[:, own:]
    for i in range(m):

        def rows(xb):
            return lambda t: ys[i, xb, pl.ds(SUB + t, half, stride=2), :]

        d2_ref[0, i] = taps_low(rows(0))
        d2_ref[1, i] = taps_low(rows(1))
        d2_ref[2, i] = taps_high(rows(0))
        d2_ref[3, i] = taps_high(rows(1))
    deeper = dot3(halves(d2_ref[0].reshape(m * half, LANES)), t3h_ref[...], t3l_ref[...])
    g_ref[...] = deeper.reshape(m, half, LANES)
    for b in range(4):
        s = [d2_ref[b, 2 * i] for i in range(m // 2)]
        d = [d2_ref[b, 2 * i + 1] for i in range(m // 2)]
        right, left = z_right(s, d), z_left(s, d)
        for j in range(2):
            pe_ref[b, j] = jnp.where(even, right[j], left[j])
            po_ref[b, j] = jnp.where(even, left[j], right[j])


def halo_lift(plane, count, got_e, got_o):
    me, first, last = place("wide")
    even = lax.rem(me, 2) == 0
    s = [plane(2 * i) for i in range(count)]
    d = [plane(2 * i + 1) for i in range(count)]
    left = [jnp.where(even, got_o(j), got_e(j)) for j in range(2)]
    right = [jnp.where(even, got_e(j), got_o(j)) for j in range(2)]
    return z_lift(s, d, left, right, first, last)


def z_one(d_ref, re_ref, ro_ref, h_ref, one_ref):
    _, nz, cl, _, _ = d_ref.shape
    m = nz // 2
    for c in range(cl):
        lanes = slice(c * LANES, (c + 1) * LANES)
        for i in range(m):
            one_ref[3, i, :, lanes] = h_ref[i, c]
        for b in range(3):
            low, high = halo_lift(
                lambda k: d_ref[b, k, c], m, lambda j: re_ref[b, j, c], lambda j: ro_ref[b, j, c]
            )
            for i in range(m):
                one_ref[b, i, :, lanes] = low[i]
                one_ref[4 + b, i, :, lanes] = high[i]


def z_two(d_ref, re_ref, ro_ref, two_ref):
    m = d_ref.shape[1] // 2
    for b in range(4):
        low, high = halo_lift(lambda k: d_ref[b, k], m, lambda j: re_ref[b, j], lambda j: ro_ref[b, j])
        for i in range(m):
            if b:
                two_ref[b - 1, i] = low[i]
            two_ref[3 + b, i] = high[i]


def near_slot(z, above):
    return jnp.where((lax.rem(z, 2) == 0) == above, 4, 12)


def pack_last(own_ref, four_ref, eight_ref, twelve_ref, px_ref, py_ref):
    me = lax.axis_index("wide")
    z = me // 4
    lanes = lax.broadcasted_iota(jnp.int32, own_ref.shape, 2)
    half = LANES // 2
    for out_ref, bit in ((px_ref, 1), (py_ref, 2)):
        above = lax.rem(me // bit, 2) == 0
        close = near_slot(z, above) == 4
        out_ref[0] = own_ref[...]
        out_ref[1] = jnp.where(close, four_ref[...], twelve_ref[...])
        rest = jnp.where(close, twelve_ref[...], four_ref[...])
        for i in range(own_ref.shape[0]):
            out_ref[2, i] = jnp.where(lanes[i] < half, rest[i], pltpu.roll(eight_ref[i], half, 1))


def mirrored(j, size):
    if isinstance(j, int):
        return -j if j < 0 else (2 * (size - 1) - j if j >= size else j)
    return jnp.where(j < 0, -j, jnp.where(j >= size, 2 * (size - 1) - j, j))


def z_deep(*refs, slots):
    got_refs = refs[: len(slots)]
    t4h_ref, t4l_ref, zz_ref, seq, low2, low3 = refs[len(slots) :]
    m, half = got_refs[0].shape[-3], zz_ref.shape[1]
    me = lax.axis_index("wide")

    def put(offset, piece):
        seq[pl.ds(lax.bitwise_xor(me, offset) * m, m)] = piece

    for ref, offsets in zip(got_refs, slots):
        if isinstance(offsets, int):
            partner = lax.bitwise_xor(me, offsets)
            above = lax.rem(partner // (1 if offsets == 1 else 2), 2) == 0
            slot = near_slot(me // 4, above)
            keep = lax.broadcasted_iota(jnp.int32, (half, LANES), 1) < LANES // 2
            put(offsets, ref[0])
            put(lax.bitwise_xor(slot, offsets), ref[1])
            for k, offset in ((0, lax.bitwise_xor(16 - slot, offsets)), (1, offsets ^ 8)):
                chip = lax.bitwise_xor(me, offset)
                for i in range(m):
                    value = pltpu.roll(ref[2, i], LANES // 2, 1) if k else ref[2, i]
                    seq[chip * m + i] = jnp.where(keep, value, 0.0)
            continue
        for k, offset in enumerate(offsets):
            put(offset, ref[k] if len(ref.shape) == 4 else ref[...])
    size = seq.shape[0]

    def at_of(ref, size, i):
        return lambda t: ref[mirrored(2 * i + t, size)]

    for i in range(size // 2):
        low2[i] = taps_low(at_of(seq, size, i))
    size2 = size // 2
    for i in range(size2 // 2):
        low3[i] = taps_low(at_of(low2, size2, i))
    own3 = m // 4
    size3 = size2 // 2
    for i in range(own3):
        zz_ref[i] = low3[me * own3 + i]
        zz_ref[own3 + i] = taps_high(at_of(low2, size2, me * own3 + i))
    for i in range(size3 // 2):
        seq[i] = taps_low(at_of(low3, size3, i))
        seq[size3 // 2 + i] = taps_high(at_of(low3, size3, i))
    rows = size3 * half
    got = dot3(halves(seq[:size3].reshape(rows, LANES)), t4h_ref[...], t4l_ref[...])
    zz_ref[2 * own3 :] = got.reshape(size3, half, LANES)


def pick(me, value, count):
    rows = value.shape[0] // count
    out = value[:rows]
    for k in range(1, count):
        out = jnp.where(me == k, value[k * rows : (k + 1) * rows], out)
    return out


def xy_deep(*refs, pair, own3):
    if pair:
        zz_ref, other_ref = refs[:2]
    else:
        zz_ref = refs[0]
    three_ref, four_ref, xs, ys = refs[2 if pair else 1 :]
    me = lax.axis_index("narrow")
    count = lax.axis_size("narrow")
    planes, rows = zz_ref.shape[-3], zz_ref.shape[-2]
    full = rows * count

    def put(value, start):
        xs[:, pl.ds(start, rows), :] = value

    if pair:
        put(zz_ref[...], pl.multiple_of(SUB + rows * me, SUB))
        put(other_ref[...], pl.multiple_of(SUB + rows * (1 - me), SUB))
    else:
        for k in range(count):
            put(zz_ref[k], SUB + rows * k)

    def fold(ref, size):
        end = SUB + size - 1
        for t in range(1, EDGE + 1):
            ref[:, SUB - t : SUB - t + 1, :] = ref[:, SUB + t : SUB + t + 1, :]
            ref[:, end + t : end + t + 1, :] = ref[:, end - t : end - t + 1, :]

    fold(xs, full)
    n3 = full // 2
    wide3 = three_ref.shape[-1]
    for k in range(2 * own3):
        bz, i = k // own3, k % own3
        at = lambda t: xs[k, pl.ds(SUB + t, n3, stride=2), :]
        for by, taps in enumerate((taps_low, taps_high)):
            mine = pick(me, taps(at), count)
            for bx in range(2):
                band = 4 * bz + 2 * by + bx
                if band:
                    three_ref[band - 1, i] = mine[:, bx * wide3 : (bx + 1) * wide3]
    for k in range(2 * own3, planes):
        at = lambda t: xs[k, pl.ds(SUB + t, n3, stride=2), :]
        ys[k - 2 * own3, SUB : SUB + n3, :] = taps_low(at)
    fold(ys, n3)
    n4 = n3 // 2
    wide4 = four_ref.shape[-1]
    deep = (planes - 2 * own3) // 2
    for k in range(2 * deep):
        bz, i = k // deep, k % deep
        at = lambda t: ys[k, pl.ds(SUB + t, n4, stride=2), :]
        for by, taps in enumerate((taps_low, taps_high)):
            mine = pick(me, taps(at), count)
            for bx in range(2):
                four_ref[4 * bz + 2 * by + bx, i] = mine[:, bx * wide4 : (bx + 1) * wide4]


def call(kernel, outs, scratch, cost=2_000_000, aliases=None):
    return pl.pallas_call(
        kernel,
        out_shape=tuple(jax.ShapeDtypeStruct(shape, F32) for shape in outs),
        out_specs=tuple(VMEM for _ in outs),
        scratch_shapes=[pltpu.VMEM(shape, F32) for shape in scratch],
        cost_estimate=pl.CostEstimate(flops=cost, bytes_accessed=cost, transcendentals=0),
        compiler_params=pltpu.CompilerParams(vmem_limit_bytes=VMEM_LIMIT),
        input_output_aliases=aliases or {},
    )


def wide_swap(value, partner):
    count, cores = lax.axis_size("wide"), lax.axis_size("narrow")
    pairs = []
    for i in range(count):
        for k in range(cores):
            j, c = (partner(i), k) if 0 <= partner(i) < count else (i, k ^ 1)
            pairs.append((i * cores + k, j * cores + c))
    return lax.ppermute(value, ("wide", "narrow"), pairs)


def even_pair(i):
    return i ^ 1


def odd_pair(i):
    return ((i + 1) ^ 1) - 1


def xor_pair(mask):
    return lambda i: i ^ mask


def gather_stages(count):
    bits = count.bit_length() - 1
    stages = []
    while bits > 0:
        take = 2 if bits >= 2 else 1
        bits -= take
        stages.append([k << bits for k in range(1, 1 << take)])
    return stages


def per_device(pressure):
    nz, ny, nx = pressure.shape
    count_y = lax.axis_size("narrow")
    count_z = lax.axis_size("wide")
    cl = nx // 2 // LANES
    own = ny // 2
    if count_y == 2:
        halos = (lax.ppermute(pressure, "narrow", [(0, 1), (1, 0)]),)
    else:
        head, tail = pressure[:, :HALO], pressure[:, ny - HALO :]
        halos = (
            lax.ppermute(tail, "narrow", [(i, i + 1) for i in range(count_y - 1)]),
            lax.ppermute(head, "narrow", [(i + 1, i) for i in range(count_y - 1)]),
        )
    table = np_split(lift_table(nx))
    padded = (nz, 2 * cl, ny + 2 * BASE, LANES)
    hbm = pl.BlockSpec(memory_space=pltpu.HBM)
    x_own, *table = pl.pallas_call(
        x_one,
        out_shape=(jax.ShapeDtypeStruct(padded, F32),)
        + tuple(jax.ShapeDtypeStruct(part.shape, part.dtype) for part in table),
        in_specs=(hbm, hbm, hbm),
        out_specs=(VMEM, VMEM, VMEM),
        scratch_shapes=[pltpu.VMEM((nz, ny, nx), F32), pltpu.SemaphoreType.DMA((PARTS + 2,))],
        cost_estimate=pl.CostEstimate(flops=2_000_000, bytes_accessed=2_000_000, transcendentals=0),
        compiler_params=pltpu.CompilerParams(vmem_limit_bytes=VMEM_LIMIT),
        name="x_one",
    )(*[pltpu.with_memory_space_constraint(v, pltpu.HBM) for v in (pressure, *table)])
    _, ll, d, le, lo, de, do = call(
        lambda *refs: xy_one(*refs, one_halo=count_y == 2),
        [
            padded,
            (nz, cl, own + SUB, LANES),
            (3, nz, cl, own, LANES),
            (2, cl, own + SUB, LANES),
            (2, cl, own + SUB, LANES),
            (3, 2, cl, own, LANES),
            (3, 2, cl, own, LANES),
        ],
        [],
        aliases={0: 0},
    )(x_own, *halos, *table)
    re = wide_swap(le, even_pair)
    ro = wide_swap(lo, odd_pair)
    rde = wide_swap(de, even_pair)
    rdo = wide_swap(do, odd_pair)
    m, half = nz // 2, own // 2
    g, d2, h, pe, po = call(
        xy_two,
        [
            (m, half, LANES),
            (4, m, half, LANES),
            (m, cl, own, LANES),
            (4, 2, half, LANES),
            (4, 2, half, LANES),
        ],
        [(m, own + SUB, cl * LANES), (m, 2, own + 2 * SUB, LANES)],
    )(ll, re, ro, *np_split(lift_table(nx // 2)), *np_split(lift_table(nx // 4)))
    pieces, slots = [g], [[0]]
    stages = gather_stages(count_z)
    for n, masks in enumerate(stages):
        final = n == len(stages) - 1
        if final and count_z == 16:
            block = (3, m, half, LANES)
            px, py = call(pack_last, [block, block], [])(*pieces)
            for mask in masks:
                pieces.append(wide_swap(px if mask == 1 else py, xor_pair(mask)))
                slots.append(mask)
            break
        whole, flat = g, [0]
        if n:
            whole = jnp.concatenate([p.reshape((-1, m, half, LANES)) for p in pieces], 0)
            flat = [o for part in slots for o in part]
        pieces = [whole]
        for mask in masks:
            pieces.append(wide_swap(whole, xor_pair(mask)))
        slots = [flat] + [[o ^ mask for o in flat] for mask in masks]
    re2 = wide_swap(pe, even_pair)
    ro2 = wide_swap(po, odd_pair)
    size = m * count_z
    own3 = m // 4
    planes = 2 * own3 + size // 4
    table4 = np.zeros((LANES, LANES))
    table4[: nx // 8, : nx // 8] = lift_table(nx // 8)
    (zz,) = call(
        lambda *refs: z_deep(*refs, slots=slots),
        [(planes, half, LANES)],
        [(size, half, LANES), (size // 2, half, LANES), (size // 4, half, LANES)],
    )(*pieces, *np_split(table4))
    (detail_one,) = call(z_one, [(7, m, own, cl * LANES)], [])(d, rde, rdo, h)
    (detail_two,) = call(z_two, [(7, m // 2, half, LANES)], [])(d2, re2, ro2)
    if count_y == 2:
        rest = (zz, lax.ppermute(zz, "narrow", [(0, 1), (1, 0)]))
    else:
        rest = (lax.all_gather(zz, "narrow"),)
    full = half * count_y
    detail_three, bands_four = call(
        lambda *refs: xy_deep(*refs, pair=count_y == 2, own3=own3),
        [(7, own3, half // 2, nx // 8), (8, size // 8, half // 4, nx // 16)],
        [(planes, full + 2 * SUB, LANES), (planes - 2 * own3, full // 2 + 2 * SUB, LANES)],
    )(*rest)
    return detail_one, detail_two, detail_three, bands_four


def solution(mesh):
    in_specs = (P("wide", "narrow", None),)
    out_specs = (
        P(None, "wide", "narrow", None),
        P(None, "wide", "narrow", None),
        P(None, "wide", "narrow", None),
        P(None, None, "narrow", None),
    )

    return jax.shard_map(per_device, mesh=mesh, in_specs=in_specs, out_specs=out_specs, check_vma=False)
```

```python
import numpy as np

import jax
import jax.numpy as jnp
from jax import lax
from jax.experimental import pallas as pl
from jax.experimental.pallas import tpu as pltpu
from jax.sharding import PartitionSpec as P


ALPHA = -1.586134342
BETA = -0.05298011854
GAMMA = 0.8829110762
DELTA = 0.4435068522
ZETA = 1.149604398

LANES = 128
SUB = 8
HALO = 16
PARTS = 1
EDGE = 4
BASE = 24
F32 = jnp.float32
VMEM_LIMIT = 16 * 1024 * 1024
VMEM = pl.BlockSpec(memory_space=pltpu.VMEM)


def lift_table(size):
    cells = np.eye(size)
    even, odd = cells[:, 0::2].copy(), cells[:, 1::2].copy()

    def ahead(v):
        return np.concatenate([v[:, 1:], v[:, -1:]], 1)

    def behind(v):
        return np.concatenate([v[:, :1], v[:, :-1]], 1)

    odd += ALPHA * (even + ahead(even))
    even += BETA * (behind(odd) + odd)
    odd += GAMMA * (even + ahead(even))
    even += DELTA * (behind(odd) + odd)
    return np.concatenate([even * ZETA, odd / ZETA], 1)


def lift_taps():
    table = lift_table(32)
    low, high = table[:, 8], table[:, 16 + 8]
    return [float(low[16 + t]) for t in range(5)], [float(high[17 + t]) for t in range(4)]


LOW, HIGH = lift_taps()


def np_split(table):
    import ml_dtypes

    whole = np.asarray(table, np.float32)
    top = whole.astype(ml_dtypes.bfloat16)
    rest = (whole - top.astype(np.float32)).astype(ml_dtypes.bfloat16)
    return jnp.asarray(top), jnp.asarray(rest)


def halves(v):
    top = v.astype(jnp.bfloat16)
    return top, (v - top.astype(F32)).astype(jnp.bfloat16)


def dot3(v, th, tl):
    top, rest = v
    return (
        jnp.dot(top, th, preferred_element_type=F32)
        + jnp.dot(top, tl, preferred_element_type=F32)
        + jnp.dot(rest, th, preferred_element_type=F32)
    )


def taps_low(at):
    return LOW[0] * at(0) + (
        (LOW[1] * (at(-1) + at(1)) + LOW[2] * (at(-2) + at(2)))
        + (LOW[3] * (at(-3) + at(3)) + LOW[4] * (at(-4) + at(4)))
    )


def taps_high(at):
    return (HIGH[0] * at(1) + HIGH[1] * (at(0) + at(2))) + (
        HIGH[2] * (at(-1) + at(3)) + HIGH[3] * (at(-2) + at(4))
    )


def taps_both(at):
    rows = {t: at(t) for t in range(-4, 5)}
    return taps_low(rows.__getitem__), taps_high(rows.__getitem__)


def z_right(s, d):
    return d[-1] + ALPHA * s[-1], s[-1] + BETA * (d[-2] + ALPHA * (s[-2] + s[-1]))


def z_left(s, d):
    return s[0], d[0] + ALPHA * (s[0] + s[1])


def z_lift(s, d, left, right, first, last):
    m = len(s)
    s0p = jnp.where(last, s[-1], right[0])
    d1 = [d[i] + ALPHA * (s[i] + (s[i + 1] if i + 1 < m else s0p)) for i in range(m)]
    d1m = jnp.where(first, d1[0], left[0] + ALPHA * s[0])
    s1 = [s[i] + BETA * ((d1[i - 1] if i else d1m) + d1[i]) for i in range(m)]
    s1p = jnp.where(last, s1[-1], s0p + BETA * (d1[-1] + right[1]))
    d2 = [d1[i] + GAMMA * (s1[i] + (s1[i + 1] if i + 1 < m else s1p)) for i in range(m)]
    s1m = left[1] + BETA * d1m
    d2m = jnp.where(first, d2[0], d1m + GAMMA * (s1m + s1[0]))
    s2 = [s1[i] + DELTA * ((d2[i - 1] if i else d2m) + d2[i]) for i in range(m)]
    return [v * ZETA for v in s2], [v * (1.0 / ZETA) for v in d2]


def place(axis):
    me, count = lax.axis_index(axis), lax.axis_size(axis)
    return me, me == 0, me == count - 1


def spread(value, th_ref, tl_ref, store):
    nz, rows, nx = value.shape
    parts = halves(value.reshape(nz * rows, nx))
    step = 2 * LANES
    for n in range(0, nx, step):
        got = dot3(parts, th_ref[:, n : n + step], tl_ref[:, n : n + step]).reshape(nz, rows, step)
        for k in range(step // LANES):
            store(n // LANES + k, got[:, :, k * LANES : (k + 1) * LANES])


def x_one(x_hbm, th_hbm, tl_hbm, xs, th_ref, tl_ref, xv, sems):
    nz, ny, _ = xv.shape
    part = nz // PARTS
    tables = [
        pltpu.make_async_copy(th_hbm, th_ref, sems.at[PARTS]),
        pltpu.make_async_copy(tl_hbm, tl_ref, sems.at[PARTS + 1]),
    ]
    pieces = [
        pltpu.make_async_copy(x_hbm.at[pl.ds(k * part, part)], xv.at[pl.ds(k * part, part)], sems.at[k])
        for k in range(PARTS)
    ]
    for copy in [pieces[0]] + tables + pieces[1:]:
        copy.start()
    for copy in tables:
        copy.wait()
    for k in range(PARTS):
        pieces[k].wait()
        planes = slice(k * part, (k + 1) * part)

        def store(chunk, block):
            xs[planes, chunk, BASE : BASE + ny, :] = block

        spread(xv[planes], th_ref, tl_ref, store)


def xy_one(*refs, one_halo):
    n_halo = 1 if one_halo else 2
    x_ref, halo_refs = refs[0], refs[1 : 1 + n_halo]
    th_ref, tl_ref, xs, ll_ref, d_ref, le_ref, lo_ref, de_ref, do_ref = refs[1 + n_halo :]
    nz, chunks, tall, _ = x_ref.shape
    ny = tall - 2 * BASE
    cl = chunks // 2
    own = ny // 2
    _, first, last = place("narrow")
    even = lax.rem(lax.axis_index("wide"), 2) == 0

    top, bottom = BASE - HALO, BASE + ny

    def store_at(starts):
        def store(chunk, block):
            for start in starts:
                xs[:, chunk, start : start + HALO, :] = block

        return store

    if one_halo:
        begin = pl.multiple_of(jnp.where(first, 0, ny - HALO), HALO)
        spread(halo_refs[0][:, pl.ds(begin, HALO), :], th_ref, tl_ref, store_at((top, bottom)))
    else:
        spread(halo_refs[0][...], th_ref, tl_ref, store_at((top,)))
        spread(halo_refs[1][...], th_ref, tl_ref, store_at((bottom,)))

    @pl.when(first)
    def _():
        for t in range(1, 13):
            upto = cl if t > EDGE else 2 * cl
            xs[:, :upto, BASE - t : BASE - t + 1, :] = xs[:, :upto, BASE + t : BASE + t + 1, :]

    end = BASE + ny - 1

    @pl.when(last)
    def _():
        for t in range(1, EDGE + 1):
            xs[:, :, end + t : end + t + 1, :] = xs[:, :, end - t : end - t + 1, :]

    upper = lax.broadcasted_iota(jnp.int32, (SUB, LANES), 0) < EDGE

    @pl.loop(0, nz)
    def _(p):
        for c in range(cl):

            def rows(chunk, start, n):
                return lambda t: xs[p, chunk, pl.ds(start + t, n, stride=2), :]

            ll_ref[p, c, :own, :], d_ref[1, p, c] = taps_both(rows(c, BASE, own))
            below = taps_low(rows(c, BASE + ny, SUB))
            above = taps_low(rows(c, BASE - 2 * SUB, SUB))
            ll_ref[p, c, own : own + SUB, :] = jnp.where(upper, below, above)
            d_ref[0, p, c], d_ref[2, p, c] = taps_both(rows(cl + c, BASE, own))

    @pl.when(last)
    def _():
        for t in range(1, EDGE + 1):
            at = own - 1
            ll_ref[:, :, at + t : at + t + 1, :] = ll_ref[:, :, at - t : at - t + 1, :]

    def edges(plane):
        s = [plane(0), plane(2), plane(nz - 4), plane(nz - 2)]
        d = [plane(1), None, plane(nz - 3), plane(nz - 1)]
        return z_right(s, d), z_left(s, d)

    for c in range(cl):
        right, left = edges(lambda k: ll_ref[k, c])
        for j in range(2):
            le_ref[j, c] = jnp.where(even, right[j], left[j])
            lo_ref[j, c] = jnp.where(even, left[j], right[j])
        for b in range(3):
            right, left = edges(lambda k: d_ref[b, k, c])
            for j in range(2):
                de_ref[b, j, c] = jnp.where(even, right[j], left[j])
                do_ref[b, j, c] = jnp.where(even, left[j], right[j])


def xy_two(ll_ref, re_ref, ro_ref, th_ref, tl_ref, t3h_ref, t3l_ref, g_ref, d2_ref, h_ref, pe_ref, po_ref, lw, ys):
    nz, cl, tall, _ = ll_ref.shape
    own = tall - SUB
    m = nz // 2
    half = own // 2
    me, first, last = place("wide")
    even = lax.rem(me, 2) == 0
    for c in range(cl):
        s = [ll_ref[2 * i, c] for i in range(m)]
        d = [ll_ref[2 * i + 1, c] for i in range(m)]
        left = [jnp.where(even, ro_ref[j, c], re_ref[j, c]) for j in range(2)]
        right = [jnp.where(even, re_ref[j, c], ro_ref[j, c]) for j in range(2)]
        low, high = z_lift(s, d, left, right, first, last)
        for i in range(m):
            lw[i, :, c * LANES : (c + 1) * LANES] = low[i]
            h_ref[i, c] = high[i][:own]
    got = dot3(halves(lw[...].reshape(m * tall, cl * LANES)), th_ref[...], tl_ref[...])
    got = got.reshape(m, tall, 2 * LANES)
    for xb in range(2):
        part = got[:, :, xb * LANES : (xb + 1) * LANES]
        ys[:, xb, SUB : SUB + own, :] = part[:, :own]
        ys[:, xb, :SUB, :] = part[:, own:]
        ys[:, xb, SUB + own : 2 * SUB + own, :] = part[:, own:]
    for i in range(m):

        def rows(xb):
            return lambda t: ys[i, xb, pl.ds(SUB + t, half, stride=2), :]

        d2_ref[0, i] = taps_low(rows(0))
        d2_ref[1, i] = taps_low(rows(1))
        d2_ref[2, i] = taps_high(rows(0))
        d2_ref[3, i] = taps_high(rows(1))
    deeper = dot3(halves(d2_ref[0].reshape(m * half, LANES)), t3h_ref[...], t3l_ref[...])
    g_ref[...] = deeper.reshape(m, half, LANES)
    for b in range(4):
        s = [d2_ref[b, 2 * i] for i in range(m // 2)]
        d = [d2_ref[b, 2 * i + 1] for i in range(m // 2)]
        right, left = z_right(s, d), z_left(s, d)
        for j in range(2):
            pe_ref[b, j] = jnp.where(even, right[j], left[j])
            po_ref[b, j] = jnp.where(even, left[j], right[j])


def halo_lift(plane, count, got_e, got_o):
    me, first, last = place("wide")
    even = lax.rem(me, 2) == 0
    s = [plane(2 * i) for i in range(count)]
    d = [plane(2 * i + 1) for i in range(count)]
    left = [jnp.where(even, got_o(j), got_e(j)) for j in range(2)]
    right = [jnp.where(even, got_e(j), got_o(j)) for j in range(2)]
    return z_lift(s, d, left, right, first, last)


def z_one(d_ref, re_ref, ro_ref, h_ref, one_ref):
    _, nz, cl, _, _ = d_ref.shape
    m = nz // 2
    for c in range(cl):
        lanes = slice(c * LANES, (c + 1) * LANES)
        for i in range(m):
            one_ref[3, i, :, lanes] = h_ref[i, c]
        for b in range(3):
            low, high = halo_lift(
                lambda k: d_ref[b, k, c], m, lambda j: re_ref[b, j, c], lambda j: ro_ref[b, j, c]
            )
            for i in range(m):
                one_ref[b, i, :, lanes] = low[i]
                one_ref[4 + b, i, :, lanes] = high[i]


def z_two(d_ref, re_ref, ro_ref, two_ref):
    m = d_ref.shape[1] // 2
    for b in range(4):
        low, high = halo_lift(lambda k: d_ref[b, k], m, lambda j: re_ref[b, j], lambda j: ro_ref[b, j])
        for i in range(m):
            if b:
                two_ref[b - 1, i] = low[i]
            two_ref[3 + b, i] = high[i]


def near_slot(z, above):
    return jnp.where((lax.rem(z, 2) == 0) == above, 4, 12)


def pack_last(own_ref, four_ref, eight_ref, twelve_ref, px_ref, py_ref):
    me = lax.axis_index("wide")
    z = me // 4
    lanes = lax.broadcasted_iota(jnp.int32, own_ref.shape, 2)
    half = LANES // 2
    for out_ref, bit in ((px_ref, 1), (py_ref, 2)):
        above = lax.rem(me // bit, 2) == 0
        close = near_slot(z, above) == 4
        out_ref[0] = own_ref[...]
        out_ref[1] = jnp.where(close, four_ref[...], twelve_ref[...])
        rest = jnp.where(close, twelve_ref[...], four_ref[...])
        for i in range(own_ref.shape[0]):
            out_ref[2, i] = jnp.where(lanes[i] < half, rest[i], pltpu.roll(eight_ref[i], half, 1))


def mirrored(j, size):
    if isinstance(j, int):
        return -j if j < 0 else (2 * (size - 1) - j if j >= size else j)
    return jnp.where(j < 0, -j, jnp.where(j >= size, 2 * (size - 1) - j, j))


def z_deep(*refs, slots):
    got_refs = refs[: len(slots)]
    t4h_ref, t4l_ref, zz_ref, seq, low2, low3 = refs[len(slots) :]
    m, half = got_refs[0].shape[-3], zz_ref.shape[1]
    me = lax.axis_index("wide")

    def put(offset, piece):
        seq[pl.ds(lax.bitwise_xor(me, offset) * m, m)] = piece

    for ref, offsets in zip(got_refs, slots):
        if isinstance(offsets, int):
            partner = lax.bitwise_xor(me, offsets)
            above = lax.rem(partner // (1 if offsets == 1 else 2), 2) == 0
            slot = near_slot(me // 4, above)
            keep = lax.broadcasted_iota(jnp.int32, (half, LANES), 1) < LANES // 2
            put(offsets, ref[0])
            put(lax.bitwise_xor(slot, offsets), ref[1])
            for k, offset in ((0, lax.bitwise_xor(16 - slot, offsets)), (1, offsets ^ 8)):
                chip = lax.bitwise_xor(me, offset)
                for i in range(m):
                    value = pltpu.roll(ref[2, i], LANES // 2, 1) if k else ref[2, i]
                    seq[chip * m + i] = jnp.where(keep, value, 0.0)
            continue
        for k, offset in enumerate(offsets):
            put(offset, ref[k] if len(ref.shape) == 4 else ref[...])
    size = seq.shape[0]

    def at_of(ref, size, i):
        return lambda t: ref[mirrored(2 * i + t, size)]

    for i in range(size // 2):
        low2[i] = taps_low(at_of(seq, size, i))
    size2 = size // 2
    for i in range(size2 // 2):
        low3[i] = taps_low(at_of(low2, size2, i))
    own3 = m // 4
    size3 = size2 // 2
    for i in range(own3):
        zz_ref[i] = low3[me * own3 + i]
        zz_ref[own3 + i] = taps_high(at_of(low2, size2, me * own3 + i))
    for i in range(size3 // 2):
        seq[i] = taps_low(at_of(low3, size3, i))
        seq[size3 // 2 + i] = taps_high(at_of(low3, size3, i))
    rows = size3 * half
    got = dot3(halves(seq[:size3].reshape(rows, LANES)), t4h_ref[...], t4l_ref[...])
    zz_ref[2 * own3 :] = got.reshape(size3, half, LANES)


def pick(me, value, count):
    rows = value.shape[0] // count
    out = value[:rows]
    for k in range(1, count):
        out = jnp.where(me == k, value[k * rows : (k + 1) * rows], out)
    return out


def xy_deep(*refs, pair, own3):
    if pair:
        zz_ref, other_ref = refs[:2]
    else:
        zz_ref = refs[0]
    three_ref, four_ref, xs, ys = refs[2 if pair else 1 :]
    me = lax.axis_index("narrow")
    count = lax.axis_size("narrow")
    planes, rows = zz_ref.shape[-3], zz_ref.shape[-2]
    full = rows * count

    def put(value, start):
        xs[:, pl.ds(start, rows), :] = value

    if pair:
        put(zz_ref[...], pl.multiple_of(SUB + rows * me, SUB))
        put(other_ref[...], pl.multiple_of(SUB + rows * (1 - me), SUB))
    else:
        for k in range(count):
            put(zz_ref[k], SUB + rows * k)

    def fold(ref, size):
        end = SUB + size - 1
        for t in range(1, EDGE + 1):
            ref[:, SUB - t : SUB - t + 1, :] = ref[:, SUB + t : SUB + t + 1, :]
            ref[:, end + t : end + t + 1, :] = ref[:, end - t : end - t + 1, :]

    fold(xs, full)
    n3 = full // 2
    wide3 = three_ref.shape[-1]
    for k in range(2 * own3):
        bz, i = k // own3, k % own3
        at = lambda t: xs[k, pl.ds(SUB + t, n3, stride=2), :]
        for by, taps in enumerate((taps_low, taps_high)):
            mine = pick(me, taps(at), count)
            for bx in range(2):
                band = 4 * bz + 2 * by + bx
                if band:
                    three_ref[band - 1, i] = mine[:, bx * wide3 : (bx + 1) * wide3]
    for k in range(2 * own3, planes):
        at = lambda t: xs[k, pl.ds(SUB + t, n3, stride=2), :]
        ys[k - 2 * own3, SUB : SUB + n3, :] = taps_low(at)
    fold(ys, n3)
    n4 = n3 // 2
    wide4 = four_ref.shape[-1]
    deep = (planes - 2 * own3) // 2
    for k in range(2 * deep):
        bz, i = k // deep, k % deep
        at = lambda t: ys[k, pl.ds(SUB + t, n4, stride=2), :]
        for by, taps in enumerate((taps_low, taps_high)):
            mine = pick(me, taps(at), count)
            for bx in range(2):
                four_ref[4 * bz + 2 * by + bx, i] = mine[:, bx * wide4 : (bx + 1) * wide4]


def call(kernel, outs, scratch, cost=2_000_000, aliases=None):
    return pl.pallas_call(
        kernel,
        out_shape=tuple(jax.ShapeDtypeStruct(shape, F32) for shape in outs),
        out_specs=tuple(VMEM for _ in outs),
        scratch_shapes=[pltpu.VMEM(shape, F32) for shape in scratch],
        cost_estimate=pl.CostEstimate(flops=cost, bytes_accessed=cost, transcendentals=0),
        compiler_params=pltpu.CompilerParams(vmem_limit_bytes=VMEM_LIMIT),
        input_output_aliases=aliases or {},
    )


def wide_swap(value, partner):
    count, cores = lax.axis_size("wide"), lax.axis_size("narrow")
    pairs = []
    for i in range(count):
        for k in range(cores):
            j, c = (partner(i), k) if 0 <= partner(i) < count else (i, k ^ 1)
            pairs.append((i * cores + k, j * cores + c))
    return lax.ppermute(value, ("wide", "narrow"), pairs)


def even_pair(i):
    return i ^ 1


def odd_pair(i):
    return ((i + 1) ^ 1) - 1


def xor_pair(mask):
    return lambda i: i ^ mask


def gather_stages(count):
    bits = count.bit_length() - 1
    stages = []
    while bits > 0:
        take = 2 if bits >= 2 else 1
        bits -= take
        stages.append([k << bits for k in range(1, 1 << take)])
    return stages


def per_device(pressure):
    nz, ny, nx = pressure.shape
    count_y = lax.axis_size("narrow")
    count_z = lax.axis_size("wide")
    cl = nx // 2 // LANES
    own = ny // 2
    if count_y == 2:
        halos = (lax.ppermute(pressure, "narrow", [(0, 1), (1, 0)]),)
    else:
        head, tail = pressure[:, :HALO], pressure[:, ny - HALO :]
        halos = (
            lax.ppermute(tail, "narrow", [(i, i + 1) for i in range(count_y - 1)]),
            lax.ppermute(head, "narrow", [(i + 1, i) for i in range(count_y - 1)]),
        )
    table = np_split(lift_table(nx))
    padded = (nz, 2 * cl, ny + 2 * BASE, LANES)
    hbm = pl.BlockSpec(memory_space=pltpu.HBM)
    x_own, *table = pl.pallas_call(
        x_one,
        out_shape=(jax.ShapeDtypeStruct(padded, F32),)
        + tuple(jax.ShapeDtypeStruct(part.shape, part.dtype) for part in table),
        in_specs=(hbm, hbm, hbm),
        out_specs=(VMEM, VMEM, VMEM),
        scratch_shapes=[pltpu.VMEM((nz, ny, nx), F32), pltpu.SemaphoreType.DMA((PARTS + 2,))],
        cost_estimate=pl.CostEstimate(flops=2_000_000, bytes_accessed=2_000_000, transcendentals=0),
        compiler_params=pltpu.CompilerParams(vmem_limit_bytes=VMEM_LIMIT),
        name="x_one",
    )(*[pltpu.with_memory_space_constraint(v, pltpu.HBM) for v in (pressure, *table)])
    _, ll, d, le, lo, de, do = call(
        lambda *refs: xy_one(*refs, one_halo=count_y == 2),
        [
            padded,
            (nz, cl, own + SUB, LANES),
            (3, nz, cl, own, LANES),
            (2, cl, own + SUB, LANES),
            (2, cl, own + SUB, LANES),
            (3, 2, cl, own, LANES),
            (3, 2, cl, own, LANES),
        ],
        [],
        aliases={0: 0},
    )(x_own, *halos, *table)
    re = wide_swap(le, even_pair)
    ro = wide_swap(lo, odd_pair)
    rde = wide_swap(de, even_pair)
    rdo = wide_swap(do, odd_pair)
    m, half = nz // 2, own // 2
    g, d2, h, pe, po = call(
        xy_two,
        [
            (m, half, LANES),
            (4, m, half, LANES),
            (m, cl, own, LANES),
            (4, 2, half, LANES),
            (4, 2, half, LANES),
        ],
        [(m, own + SUB, cl * LANES), (m, 2, own + 2 * SUB, LANES)],
    )(ll, re, ro, *np_split(lift_table(nx // 2)), *np_split(lift_table(nx // 4)))
    pieces, slots = [g], [[0]]
    stages = gather_stages(count_z)
    for n, masks in enumerate(stages):
        final = n == len(stages) - 1
        if final and count_z == 16:
            block = (3, m, half, LANES)
            px, py = call(pack_last, [block, block], [])(*pieces)
            for mask in masks:
                pieces.append(wide_swap(px if mask == 1 else py, xor_pair(mask)))
                slots.append(mask)
            break
        whole, flat = g, [0]
        if n:
            whole = jnp.concatenate([p.reshape((-1, m, half, LANES)) for p in pieces], 0)
            flat = [o for part in slots for o in part]
        pieces = [whole]
        for mask in masks:
            pieces.append(wide_swap(whole, xor_pair(mask)))
        slots = [flat] + [[o ^ mask for o in flat] for mask in masks]
    re2 = wide_swap(pe, even_pair)
    ro2 = wide_swap(po, odd_pair)
    size = m * count_z
    own3 = m // 4
    planes = 2 * own3 + size // 4
    table4 = np.zeros((LANES, LANES))
    table4[: nx // 8, : nx // 8] = lift_table(nx // 8)
    (zz,) = call(
        lambda *refs: z_deep(*refs, slots=slots),
        [(planes, half, LANES)],
        [(size, half, LANES), (size // 2, half, LANES), (size // 4, half, LANES)],
    )(*pieces, *np_split(table4))
    (detail_one,) = call(z_one, [(7, m, own, cl * LANES)], [])(d, rde, rdo, h)
    (detail_two,) = call(z_two, [(7, m // 2, half, LANES)], [])(d2, re2, ro2)
    if count_y == 2:
        rest = (zz, lax.ppermute(zz, "narrow", [(0, 1), (1, 0)]))
    else:
        rest = (lax.all_gather(zz, "narrow"),)
    full = half * count_y
    detail_three, bands_four = call(
        lambda *refs: xy_deep(*refs, pair=count_y == 2, own3=own3),
        [(7, own3, half // 2, nx // 8), (8, size // 8, half // 4, nx // 16)],
        [(planes, full + 2 * SUB, LANES), (planes - 2 * own3, full // 2 + 2 * SUB, LANES)],
    )(*rest)
    return detail_one, detail_two, detail_three, bands_four


def solution(mesh):
    in_specs = (P("wide", "narrow", None),)
    out_specs = (
        P(None, "wide", "narrow", None),
        P(None, "wide", "narrow", None),
        P(None, "wide", "narrow", None),
        P(None, None, "narrow", None),
    )

    return jax.shard_map(per_device, mesh=mesh, in_specs=in_specs, out_specs=out_specs, check_vma=False)
```
